128 devices in a mesh: guide: 2 (over core), tensor: 16 (over y, x), batch: 4 (over z).
Axes of the slice: x: 4, y: 4, z: 4, core: 2. Of those that a mesh axis runs over, the one named last changes fastest.
Arguments:
- stream: bfloat16 [2, 512, 2048], P('guide', ('batch', 'tensor')), may hold values from -6 to 6
- attn_gain: float32 [2048], replicated, may hold values from 0.25 to 1.75
- w_qkv: bfloat16 [2048, 3072], P(None, 'tensor'), may hold values from -0.125 to 0.125
- cache_keys: bfloat16 [2, 512, 1024, 512], P('guide', ('batch', 'tensor')), may hold values from -600 to 600
- cache_values: bfloat16 [2, 512, 1024, 512], P('guide', ('batch', 'tensor')), may hold values from -6 to 6
- cache_len: int32 [2, 512], P('guide', ('batch', 'tensor')), may hold values from 1 to 1024, as said below
- w_out: bfloat16 [2048, 2048], P('tensor'), may hold values from -0.125 to 0.125
- mlp_gain: float32 [2048], replicated, may hold values from 0.25 to 1.75
- w_gate: bfloat16 [2048, 8192], P(None, 'tensor'), may hold values from -0.125 to 0.125
- w_up: bfloat16 [2048, 8192], P(None, 'tensor'), may hold values from -0.125 to 0.125
- w_down: bfloat16 [8192, 2048], P('tensor'), may hold values from -0.0625 to 0.0625
- final_gain: float32 [2048], replicated, may hold values from 0.25 to 1.75
- lm_head: bfloat16 [65536, 2048], P(('guide', 'tensor')), may hold values from -128 to 128
- next_gain: float32 [2048], replicated, may hold values from 0.25 to 1.75
- w_next: bfloat16 [2048, 3072], P(None, 'tensor'), may hold values from -0.125 to 0.125
- tenant_counts: int32 [4], replicated, may hold values from 1 to 256, 512 in all
- guide_level: int32 [4], replicated, may hold values from 4 to 16
Outputs:
- logprobs: float32 [512, 65536], P('batch', ('guide', 'tensor'))
- layer_out: bfloat16 [2, 512, 2048], P('guide', ('batch', 'tensor'))
- next_qkv: bfloat16 [2, 512, 3072], P('guide', 'batch', 'tensor')
The draws below stay inside these ranges and needn't reach their ends.
Inputs may be any that keep to these rules, and one draw needn't show every extreme that they name: `cache_len`: in each branch some request has 1024 cached tokens.
All inputs are finite; a program needn't handle non-finite values.
Results may differ from the reference program's by a relative error of at most 0.024.
Values may be sent and summed in bfloat16 or wider, within the bound.
A program may use at most 128 MiB of HBM per device.

```python
import math
import jax
import jax.numpy as jnp
import numpy as np
from jax import lax

D = 2048
HEADS = 32
KV_HEADS = 8
HEAD_DIM = 64
FF = 8192
VOCAB = 65536
TENANTS = 4
CACHE_LEN = 1024
QKV_COLS = 3072
REQUESTS = 512


def cache_lengths(key):
    folded = jax.random.fold_in(key, 11)
    first_key, second_key, third_key = jax.random.split(folded, 3)
    base_len = jax.random.randint(first_key, (2, REQUESTS), 1, CACHE_LEN + 1)
    shifts = jax.random.randint(second_key, (2, REQUESTS), 0, 3) + jnp.array([[0], [1]], dtype=jnp.int32)
    lengths = jnp.maximum(jnp.right_shift(base_len, shifts), 1)
    longest = jax.random.randint(third_key, (2,), 0, REQUESTS)
    lengths = lengths.at[jnp.arange(2), longest].set(CACHE_LEN)
    return lengths.astype(jnp.int32)


def draw_cache_len(key, part):
    return cache_lengths(key)


def draw_cache_keys(key, part):
    folded = jax.random.fold_in(key, 23)
    normal_key = jax.random.fold_in(folded, 0)
    base_keys = jax.random.normal(normal_key, (2, REQUESTS, CACHE_LEN, KV_HEADS * HEAD_DIM), jnp.float32)
    return jnp.clip(base_keys, -600.0, 600.0).astype(jnp.bfloat16)


def draw_lm_head(key, part):
    folded = jax.random.fold_in(key, 37)
    normal_key, scale_key = jax.random.split(folded, 2)
    rows_up = jnp.arange(VOCAB, dtype=jnp.float32)[:, None] / VOCAB
    spread = jnp.exp(jax.random.uniform(scale_key, (VOCAB, 1), jnp.float32) * math.log(10.0))
    weights = jax.random.normal(normal_key, (VOCAB, D), jnp.float32) * (3.0 / math.sqrt(D)) * spread * (0.5 + rows_up) * 0.5
    return jnp.clip(weights, -128.0, 128.0).astype(jnp.bfloat16)


def with_ends(values, rng, smallest, top_value):
    shape = values.shape
    index_at = [jax.random.randint(jax.random.fold_in(rng, axis), (), 0, shape[axis]) for axis in range(len(shape))]
    values = values.at[tuple(index_at)].set(smallest)
    longest = shape.index(max(shape))
    index_at[longest] = (index_at[longest] + 1) % shape[longest]
    return values.at[tuple(index_at)].set(top_value)


def steps_of(rng, extent, shards, low, top_value):
    def one(axis_at, shards_of):
        steps = jax.random.uniform(jax.random.fold_in(jax.random.fold_in(rng, 6), axis_at), (shards_of,), jnp.float32, low / len(shards), top_value / len(shards))
        return jnp.repeat(jnp.exp(steps), extent[axis_at] // shards_of).reshape((-1,) + (1,) * (len(extent) - axis_at - 1))

    level = one(*shards[0])
    for cut in shards[1:]:
        level = level * one(*cut)
    return level


def split_up(count, total, bound, lean):
    weights = [(1 << 20) // math.isqrt(standing ** lean) + 1 for standing in range(2, count + 1)]
    surplus, counts = total - bound - (count - 1), [1] * (count - 1)
    while surplus > 0:
        movable = [i for i in range(count - 1) if counts[i] < bound]
        whole, budget = sum([weights[i] for i in movable]), surplus
        for i in movable:
            extra = min(bound - counts[i], max(1, budget * weights[i] // whole), surplus)
            counts[i] = counts[i] + extra
            surplus = surplus - extra
    return np.array([bound] + counts)


def uneven_parts(key, amount, total, reach, slope):
    if amount == 2:
        one = jax.random.randint(key, (), max(1, total - reach), min(reach, total - 1) + 1)
        return jnp.stack([one, total - one])
    sizes = jnp.asarray(split_up(amount, total, reach, slope), jnp.int32)
    pairs = (amount - 1) // 2
    source_of, sink = sizes[1:1 + 2 * pairs:2], sizes[2:2 + 2 * pairs:2]
    margin = jnp.minimum(source_of - 1, reach - sink)
    moved = jax.random.randint(jax.random.fold_in(key, 1), (pairs,), 0, 1 << 20) % (margin + 1)
    sizes = sizes.at[1:1 + 2 * pairs:2].set(source_of - moved).at[2:2 + 2 * pairs:2].set(sink + moved)
    return sizes[jax.random.permutation(jax.random.fold_in(key, 2), amount)]


def normal_values(own_key, extent, scale, bound, cuts=(), kind=jnp.bfloat16):
    result = scale * jax.random.normal(own_key, extent, jnp.float32)
    if cuts:
        result = result * steps_of(own_key, extent, cuts, -0.22, 0.18)
    return jnp.clip(result, -bound, bound).astype(kind)


def setup_inputs(seed: int = 0) -> dict:
    streams_of = jax.random.split(jax.random.key(seed), 18)
    return {
        "stream": normal_values(streams_of[0], (2, REQUESTS, D), 1.0, 6.0, ((0, 2), (1, 64))),
        "attn_gain": jnp.clip(1.0 + 0.15 * jax.random.normal(streams_of[1], (D,), jnp.float32), 0.25, 1.75),
        "w_qkv": normal_values(streams_of[2], (D, QKV_COLS), D ** -0.5, 0.125, ((1, 16),)),
        "cache_keys": draw_cache_keys(jax.random.fold_in(streams_of[17], 71), 0),
        "cache_values": normal_values(streams_of[4], (2, REQUESTS, CACHE_LEN, KV_HEADS * HEAD_DIM), 1.0, 6.0, ((0, 2), (1, 64))),
        "cache_len": draw_cache_len(jax.random.fold_in(streams_of[17], 71), 0),
        "w_out": normal_values(streams_of[6], (D, D), D ** -0.5, 0.125, ((0, 16),)),
        "mlp_gain": jnp.clip(1.0 + 0.15 * jax.random.normal(streams_of[7], (D,), jnp.float32), 0.25, 1.75),
        "w_gate": normal_values(streams_of[8], (D, FF), D ** -0.5, 0.125, ((1, 16),)),
        "w_up": normal_values(streams_of[9], (D, FF), D ** -0.5, 0.125, ((1, 16),)),
        "w_down": normal_values(streams_of[10], (FF, D), FF ** -0.5, 0.0625, ((0, 16),)),
        "final_gain": jnp.clip(1.0 + 0.15 * jax.random.normal(streams_of[11], (D,), jnp.float32), 0.25, 1.75),
        "lm_head": draw_lm_head(jax.random.fold_in(streams_of[17], 71), 0),
        "next_gain": jnp.clip(1.0 + 0.15 * jax.random.normal(streams_of[13], (D,), jnp.float32), 0.25, 1.75),
        "w_next": normal_values(streams_of[14], (D, QKV_COLS), D ** -0.5, 0.125, ((1, 16),)),
        "tenant_counts": uneven_parts(streams_of[15], TENANTS, REQUESTS, REQUESTS // 2, 2).astype(jnp.int32),
        "guide_level": with_ends(jax.random.randint(streams_of[16], (TENANTS,), 4, 17), jax.random.fold_in(streams_of[16], 1), 4, 16).astype(jnp.int32),
    }


EPSILON = 1e-05
ROPE_BASE = 500000.0
MASKED = -1e+30

def rms_norm(values, gain):
    widened = values.astype(jnp.float32)
    factor = lax.rsqrt(lax.optimization_barrier(jnp.mean(widened * widened, axis=-1, keepdims=True)) + EPSILON)
    return (widened * factor * gain).astype(jnp.bfloat16)

def scaled_freq(head_size):
    half_dim = head_size // 2
    steps_up = jnp.arange(half_dim, dtype=jnp.float32)
    base_freq = jnp.exp(steps_up * (-2.0 * math.log(ROPE_BASE) / head_size))
    wavelen = 2.0 * math.pi / base_freq
    smooth = (8192.0 / wavelen - 1.0) / 3.0
    middle = (1.0 - smooth) * base_freq / 32.0 + smooth * base_freq
    return jnp.where(wavelen < 2048.0, base_freq, jnp.where(wavelen > 8192.0, base_freq / 32.0, middle))

def rotate(values, position):
    half_dim = values.shape[-1] // 2
    freq = scaled_freq(values.shape[-1])
    angle = position * freq
    cosine = jnp.cos(angle)
    sine = jnp.sin(angle)
    first = values[..., :half_dim].astype(jnp.float32)
    second = values[..., half_dim:].astype(jnp.float32)
    joined = jnp.concatenate([first * cosine - second * sine, second * cosine + first * sine], axis=-1)
    return joined.astype(jnp.bfloat16)

def widen(values):
    return lax.optimization_barrier(values).astype(jnp.float32)

def attend_one(item):
    query, new_key, new_value, keys, values, length = item
    per_group = HEADS // KV_HEADS
    scale = HEAD_DIM ** (-0.5)
    query_f = widen(query).reshape(KV_HEADS, per_group, HEAD_DIM)
    keys_f = keys.astype(jnp.float32).reshape(CACHE_LEN, KV_HEADS, HEAD_DIM)
    values_f = values.astype(jnp.float32).reshape(CACHE_LEN, KV_HEADS, HEAD_DIM)
    live_mask = jnp.arange(CACHE_LEN, dtype=jnp.int32) < length
    scores = jnp.einsum('kgd,lkd->kgl', query_f, keys_f) * scale
    scores = jnp.where(live_mask, scores, MASKED)
    fresh = jnp.einsum('kgd,kd->kg', query_f, widen(new_key)) * scale
    peak = jnp.maximum(lax.optimization_barrier(jnp.max(scores, axis=-1)), fresh)
    expd = jnp.where(live_mask, jnp.exp(scores - peak[..., None]), 0.0)
    fresh_exp = jnp.exp(fresh - peak)
    total = lax.optimization_barrier(jnp.sum(expd, axis=-1)) + fresh_exp
    weighted = jnp.einsum('kgl,lkd->kgd', widen(expd.astype(jnp.bfloat16)), values_f)
    weighted = weighted + widen(fresh_exp.astype(jnp.bfloat16))[..., None] * widen(new_value)[:, None, :]
    return (weighted / total[..., None]).reshape(HEADS * HEAD_DIM).astype(jnp.bfloat16)

def reference(stream, attn_gain, w_qkv, cache_keys, cache_values, cache_len, w_out, mlp_gain, w_gate, w_up, w_down, final_gain, lm_head, next_gain, w_next, tenant_counts, guide_level):
    flat = stream.reshape(2 * REQUESTS, D)
    kv_width = KV_HEADS * HEAD_DIM
    normed = rms_norm(flat, attn_gain)
    projected = jnp.dot(normed, w_qkv, preferred_element_type=jnp.float32).astype(jnp.bfloat16)
    lengths = cache_len.reshape(2 * REQUESTS).astype(jnp.int32)
    position = lengths.astype(jnp.float32)[:, None, None]
    queries = rotate(projected[:, :D].reshape(2 * REQUESTS, HEADS, HEAD_DIM), position)
    new_keys = rotate(projected[:, D:D + kv_width].reshape(2 * REQUESTS, KV_HEADS, HEAD_DIM), position)
    new_values = projected[:, D + kv_width:].reshape(2 * REQUESTS, KV_HEADS, HEAD_DIM)
    mixed = lax.map(attend_one, (queries, new_keys, new_values, cache_keys.reshape(2 * REQUESTS, CACHE_LEN, kv_width), cache_values.reshape(2 * REQUESTS, CACHE_LEN, kv_width), lengths))
    attn_terms = jnp.dot(mixed, w_out, preferred_element_type=jnp.float32)
    after_attn = (flat.astype(jnp.float32) + attn_terms).astype(jnp.bfloat16)
    normed_mlp = rms_norm(after_attn, mlp_gain)
    gate = jnp.dot(normed_mlp, w_gate, preferred_element_type=jnp.float32)
    upward = jnp.dot(normed_mlp, w_up, preferred_element_type=jnp.float32)
    hidden = (jax.nn.silu(gate) * upward).astype(jnp.bfloat16)
    down_terms = jnp.dot(hidden, w_down, preferred_element_type=jnp.float32)
    layer_out = (after_attn.astype(jnp.float32) + down_terms).astype(jnp.bfloat16)
    next_qkv = jnp.dot(rms_norm(layer_out, next_gain), w_next, preferred_element_type=jnp.float32).astype(jnp.bfloat16)
    final = rms_norm(layer_out, final_gain)
    logits = lax.dot_general(final, lm_head, (((1,), (1,)), ((), ())), preferred_element_type=jnp.float32)
    logits = logits.reshape(2, REQUESTS, VOCAB)
    bounds = jnp.cumsum(tenant_counts.astype(jnp.int32))[:-1]
    request_ids = jnp.arange(REQUESTS, dtype=jnp.int32)
    tenant = lax.optimization_barrier(jnp.sum((request_ids[:, None] >= bounds[None, :]).astype(jnp.int32), axis=1))
    chosen = (tenant[:, None] == jnp.arange(TENANTS, dtype=jnp.int32)[None, :]).astype(jnp.float32)
    weight = lax.optimization_barrier(jnp.sum(chosen * guide_level.astype(jnp.float32)[None, :], axis=1)) * 0.25
    guided = logits[1] + weight[:, None] * (logits[0] - logits[1])
    peak = lax.optimization_barrier(jnp.max(guided, axis=1, keepdims=True))
    mass = lax.optimization_barrier(jnp.sum(jnp.exp(guided - peak), axis=1, keepdims=True))
    logprobs = guided - peak - jnp.log(mass)
    return (logprobs, layer_out.reshape(2, REQUESTS, D), next_qkv.reshape(2, REQUESTS, QKV_COLS))
```

```python
import functools
import math

import jax
import jax.numpy as jnp
from jax import lax
from jax.experimental import pallas as pl
from jax.experimental.pallas import tpu as pltpu
from jax.sharding import PartitionSpec as P

D = 2048
HALF = D // 2
HEADS = 32
KV_HEADS = 8
GROUPS = HEADS // KV_HEADS
HEAD_DIM = 64
KV_WIDTH = KV_HEADS * HEAD_DIM
TENANTS = 4
SLOTS = 1024
FF_LOCAL = 512
QKV_LOCAL = 192
VOCAB_LOCAL = 2048
ROWS = 128
OWN = 8
SIDE = 4
TENSOR = 16
GUIDE = 2
VOCAB_STEP = 256

EPSILON = 1e-05
ROPE_BASE = 500000.0
MASKED = -1e30
MESH = pl.DeviceIdType.MESH
F32 = jnp.float32
BF16 = jnp.bfloat16
LOW = pl.ds(0, HALF)
HIGH = pl.ds(HALF, HALF)
NT = (((1,), (1,)), ((), ()))


def norm_factor(wide):
    return lax.rsqrt(jnp.mean(wide * wide, axis=-1, keepdims=True) + EPSILON)


def rms_norm(wide, gain):
    return wide * norm_factor(wide) * gain


def lane_freq(shape):
    lane = lax.broadcasted_iota(jnp.int32, shape, 1)
    steps_up = (lane % (HEAD_DIM // 2)).astype(F32)
    base_freq = jnp.exp(steps_up * (-2.0 * math.log(ROPE_BASE) / HEAD_DIM))
    wavelen = 2.0 * math.pi / base_freq
    smooth = (8192.0 / wavelen - 1.0) / 3.0
    middle = (1.0 - smooth) * base_freq / 32.0 + smooth * base_freq
    return jnp.where(
        wavelen < 2048.0, base_freq, jnp.where(wavelen > 8192.0, base_freq / 32.0, middle)
    )


def rotate(wide, cosine, sine, first):
    width = wide.shape[-1]
    ahead = pltpu.roll(wide, width - HEAD_DIM // 2, 1)
    behind = pltpu.roll(wide, HEAD_DIM // 2, 1)
    return wide * cosine + jnp.where(first, -ahead, behind) * sine


def spread(block):
    return block.astype(F32).reshape(-1, block.shape[-1]).astype(BF16)


def drain(ref, sem):
    pltpu.make_async_copy(ref, ref, sem).wait()


def send(src, dst, send_sem, recv_sem, device):
    pltpu.make_async_remote_copy(
        src_ref=src,
        dst_ref=dst,
        send_sem=send_sem,
        recv_sem=recv_sem,
        device_id=device,
        device_id_type=MESH,
    ).start()


def gather_first(buf, y, x, sends, recvs):
    for step in (2, 1, 3):
        there = lax.rem(x + step, SIDE)
        own = buf.at[y, x, :, LOW]
        send(own, own, sends.at[0], recvs.at[0], {"tensor": y * SIDE + there})
        there = lax.rem(y + step, SIDE)
        own = buf.at[y, x, :, HIGH]
        send(own, own, sends.at[1], recvs.at[1], {"tensor": there * SIDE + x})


def gather_second(buf, y, x, sends, recvs):
    part = buf.at[0, pl.ds(0, SIDE - 1), :, LOW]
    drain(part, recvs.at[0])
    for step in (2, 1, 3):
        there = lax.rem(y + step, SIDE)
        row = buf.at[y, :, :, LOW]
        send(row, row, sends.at[2], recvs.at[2], {"tensor": there * SIDE + x})
    drain(part, recvs.at[1])
    for step in (2, 1, 3):
        there = lax.rem(x + step, SIDE)
        column = buf.at[:, x, :, HIGH]
        send(column, column, sends.at[3], recvs.at[3], {"tensor": y * SIDE + there})


def gather_low(buf, recvs):
    drain(buf.at[pl.ds(0, SIDE - 1), :, :, LOW], recvs.at[2])


def gather_high(buf, recvs):
    drain(buf.at[pl.ds(0, SIDE - 1), :, :, LOW], recvs.at[3])


def gather_sent(buf, sends):
    part = buf.at[0, pl.ds(0, SIDE - 1), :, LOW]
    drain(part, sends.at[0])
    drain(part, sends.at[1])
    whole = buf.at[pl.ds(0, SIDE - 1), :, :, LOW]
    drain(whole, sends.at[2])
    drain(whole, sends.at[3])


def all_gather(buf, y, x, sends, recvs):
    gather_first(buf, y, x, sends, recvs)
    gather_second(buf, y, x, sends, recvs)
    gather_low(buf, recvs)
    gather_high(buf, recvs)


def reduce_scatter(partial, first_low, first_high, mid_low, mid_high, last_low, last_high, y, x, sends, recvs):
    for step in (2, 1, 3):
        there = lax.rem(x + step, SIDE)
        send(
            partial.at[:, there, :, LOW], first_low.at[step - 1], sends.at[0], recvs.at[0],
            {"tensor": y * SIDE + there},
        )
        there = lax.rem(y + step, SIDE)
        send(
            partial.at[there, :, :, HIGH], first_high.at[step - 1], sends.at[1], recvs.at[1],
            {"tensor": there * SIDE + x},
        )
    drain(first_low, recvs.at[0])
    for at in range(SIDE):
        part = partial[at, x, :, LOW].astype(F32)
        for k in range(SIDE - 1):
            part = part + first_low[k, at].astype(F32)
        mid_low[at] = part.astype(BF16)
    for step in (2, 1, 3):
        there = lax.rem(y + step, SIDE)
        send(
            mid_low.at[there], last_low.at[step - 1], sends.at[2], recvs.at[2],
            {"tensor": there * SIDE + x},
        )
    drain(first_high, recvs.at[1])
    for at in range(SIDE):
        part = partial[y, at, :, HIGH].astype(F32)
        for k in range(SIDE - 1):
            part = part + first_high[k, at].astype(F32)
        mid_high[at] = part.astype(BF16)
    for step in (2, 1, 3):
        there = lax.rem(x + step, SIDE)
        send(
            mid_high.at[there], last_high.at[step - 1], sends.at[3], recvs.at[3],
            {"tensor": y * SIDE + there},
        )
    drain(last_low, recvs.at[2])
    low = mid_low[y].astype(F32)
    for k in range(SIDE - 1):
        low = low + last_low[k].astype(F32)
    drain(last_high, recvs.at[3])
    high = mid_high[x].astype(F32)
    for k in range(SIDE - 1):
        high = high + last_high[k].astype(F32)
    return jnp.concatenate([low, high], axis=1)


def scatter_sent(first_low, first_high, last_low, last_high, sends):
    drain(first_low, sends.at[0])
    drain(first_high, sends.at[1])
    drain(last_low, sends.at[2])
    drain(last_high, sends.at[3])


def exchange(src, dst, me, send_sem, recv_sem):
    dst[me] = src[me]
    for step in range(1, TENSOR):
        there = lax.rem(me + step, TENSOR)
        send(src.at[there], dst.at[me], send_sem, recv_sem, {"tensor": there})


def kernel(
    stream, attn_gain, w_qkv, keys, values, lengths, w_out, mlp_gain, w_gate, w_up, w_down,
    final_gain, lm_head, next_gain, w_next, counts, levels,
    logprobs, layer_out, next_qkv,
    stream_v, gains_v, w_qkv_v, keys_v, values_v, w_out_v, w_gate_v, w_up_v, w_down_v, lm_head_v, w_next_v,
    gather_a, gather_b, gather_c, other_c, proj, request_side, queries, mixed, head_out, head_in,
    partial, first_low, first_high, mid_low, mid_high, last_low, last_high,
    final_rows, next_rows, stats_own, stats_all,
    load_sems, ag_send, ag_recv, rs_send, rs_recv, a2a_send, a2a_recv, pair_send, pair_recv,
):
    guide = lax.axis_index("guide")
    me = lax.axis_index("tensor")
    batch = lax.axis_index("batch")
    y = me // SIDE
    x = lax.rem(me, SIDE)
    other = 1 - guide

    loads = [
        pltpu.make_async_copy(stream.at[0], stream_v, load_sems.at[0]),
        pltpu.make_async_copy(attn_gain, gains_v.at[0], load_sems.at[1]),
        pltpu.make_async_copy(w_qkv, w_qkv_v, load_sems.at[2]),
        pltpu.make_async_copy(keys.at[0], keys_v, load_sems.at[3]),
        pltpu.make_async_copy(values.at[0], values_v, load_sems.at[4]),
        pltpu.make_async_copy(w_out, w_out_v, load_sems.at[5]),
        pltpu.make_async_copy(mlp_gain, gains_v.at[1], load_sems.at[6]),
        pltpu.make_async_copy(w_gate, w_gate_v, load_sems.at[7]),
        pltpu.make_async_copy(w_up, w_up_v, load_sems.at[8]),
        pltpu.make_async_copy(w_down, w_down_v, load_sems.at[9]),
        pltpu.make_async_copy(next_gain, gains_v.at[2], load_sems.at[10]),
        pltpu.make_async_copy(final_gain, gains_v.at[3], load_sems.at[11]),
        pltpu.make_async_copy(w_next, w_next_v, load_sems.at[12]),
        pltpu.make_async_copy(lm_head, lm_head_v, load_sems.at[13]),
    ]
    for load in loads:
        load.start()

    barrier = pltpu.get_barrier_semaphore()
    for step in range(1, TENSOR):
        there = lax.rem(me + step, TENSOR)
        pl.semaphore_signal(barrier, inc=1, device_id={"tensor": there}, device_id_type=MESH)
    for there in range(TENSOR):
        pl.semaphore_signal(
            barrier, inc=1, device_id={"guide": other, "tensor": there}, device_id_type=MESH
        )

    loads[0].wait()
    loads[1].wait()
    own_rows = stream_v[...].astype(F32)
    gather_a[y, x] = rms_norm(own_rows, gains_v[0]).astype(BF16)
    pl.semaphore_wait(barrier, 2 * TENSOR - 1)

    gather_first(gather_a, y, x, ag_send.at[0], ag_recv.at[0])
    row = lax.broadcasted_iota(jnp.int32, (OWN, 2 * HEAD_DIM), 0)
    position = jnp.zeros((OWN, 2 * HEAD_DIM), F32)
    for r in range(OWN):
        position = jnp.where(row == r, lengths[0, r].astype(F32), position)
    angle = position * lane_freq((OWN, 2 * HEAD_DIM))
    cosine = jnp.concatenate([jnp.cos(angle)] * (KV_WIDTH // (2 * HEAD_DIM)), axis=1)
    sine = jnp.concatenate([jnp.sin(angle)] * (KV_WIDTH // (2 * HEAD_DIM)), axis=1)
    gather_second(gather_a, y, x, ag_send.at[0], ag_recv.at[0])
    loads[2].wait()
    gather_low(gather_a, ag_recv.at[0])
    gather_high(gather_a, ag_recv.at[0])

    rows = spread(gather_a[...])
    projected = jnp.dot(rows, w_qkv_v[...], preferred_element_type=F32)
    proj[:, :, 0:QKV_LOCAL] = projected.reshape(TENSOR, OWN, QKV_LOCAL).astype(BF16)
    exchange(proj, request_side, me, a2a_send.at[0], a2a_recv.at[0])
    drain(request_side.at[pl.ds(0, TENSOR - 1)], a2a_recv.at[0])

    def piece(column):
        at, j = divmod(column, 3)
        return request_side[at, :, j * HEAD_DIM : (j + 1) * HEAD_DIM].astype(F32)

    lane = lax.broadcasted_iota(jnp.int32, (OWN, KV_WIDTH), 1)
    first = lax.rem(lane, HEAD_DIM) < HEAD_DIM // 2
    for g in range(GROUPS):
        wide = jnp.concatenate([piece(GROUPS * k + g) for k in range(KV_HEADS)], axis=1)
        queries[g] = rotate(wide, cosine, sine, first).astype(BF16).astype(F32) * (HEAD_DIM**-0.5)
    wide = jnp.concatenate([piece(HEADS + k) for k in range(KV_HEADS)], axis=1)
    queries[GROUPS] = rotate(wide, cosine, sine, first).astype(BF16).astype(F32)
    queries[GROUPS + 1] = jnp.concatenate(
        [piece(HEADS + KV_HEADS + k) for k in range(KV_HEADS)], axis=1
    )

    loads[3].wait()
    loads[4].wait()
    own_head = lane // HEAD_DIM == lax.broadcasted_iota(jnp.int32, (OWN, KV_WIDTH), 0)
    slot = lax.broadcasted_iota(jnp.int32, (HEADS, SLOTS), 1)

    def attend(r, carry):
        rowed = [
            jnp.where(own_head, jnp.broadcast_to(queries[g, pl.ds(r, 1), :], (KV_HEADS, KV_WIDTH)), 0.0)
            for g in range(GROUPS)
        ]
        spread_q = jnp.concatenate(rowed, axis=0)
        new_key = queries[GROUPS, pl.ds(r, 1), :]
        new_value = queries[GROUPS + 1, pl.ds(r, 1), :]
        scores = lax.dot_general(spread_q.astype(BF16), keys_v[r], NT, preferred_element_type=F32)
        fresh = jnp.sum(spread_q * new_key, axis=1, keepdims=True)
        scores = jnp.where(slot < lengths[0, r], scores, MASKED)
        peak = jnp.maximum(jnp.max(scores, axis=1, keepdims=True), fresh)
        expd = jnp.exp(scores - peak)
        fresh_exp = jnp.exp(fresh - peak)
        total = jnp.sum(expd, axis=1, keepdims=True) + fresh_exp
        weighted = jnp.dot(expd.astype(BF16), values_v[r], preferred_element_type=F32)
        weighted = weighted + fresh_exp.astype(BF16).astype(F32) * new_value
        weighted = weighted / total
        for g in range(GROUPS):
            kept = jnp.where(own_head, weighted[g * KV_HEADS : (g + 1) * KV_HEADS], 0.0)
            mixed[g, pl.ds(r, 1), :] = jnp.sum(kept, axis=0, keepdims=True)
        return carry

    lax.fori_loop(0, OWN, attend, 0, unroll=True)

    for at in range(TENSOR):
        k, g = at // 2, (at % 2) * 2
        here = slice(k * HEAD_DIM, (k + 1) * HEAD_DIM)
        head_out[at] = jnp.concatenate([mixed[g, :, here], mixed[g + 1, :, here]], axis=1).astype(BF16)
    exchange(head_out, head_in, me, a2a_send.at[1], a2a_recv.at[1])
    loads[5].wait()
    drain(head_in.at[pl.ds(0, TENSOR - 1)], a2a_recv.at[1])

    terms = jnp.dot(spread(head_in[...]), w_out_v[...], preferred_element_type=F32)
    partial[0] = terms.reshape(SIDE, SIDE, OWN, D).astype(BF16)
    attn_share = reduce_scatter(
        partial.at[0], first_low.at[0], first_high.at[0], mid_low.at[0], mid_high.at[0],
        last_low.at[0], last_high.at[0], y, x, rs_send.at[0], rs_recv.at[0],
    )
    after_attn = (own_rows + attn_share).astype(BF16).astype(F32)
    loads[6].wait()
    gather_b[y, x] = rms_norm(after_attn, gains_v[1]).astype(BF16)
    gather_first(gather_b, y, x, ag_send.at[1], ag_recv.at[1])
    gather_second(gather_b, y, x, ag_send.at[1], ag_recv.at[1])
    for load in loads[7:10]:
        load.wait()
    gather_low(gather_b, ag_recv.at[1])
    gather_high(gather_b, ag_recv.at[1])

    rows = spread(gather_b[...])
    gate = jnp.dot(rows, w_gate_v[...], preferred_element_type=F32)
    upward = jnp.dot(rows, w_up_v[...], preferred_element_type=F32)
    hidden = (gate * jax.nn.sigmoid(gate) * upward).astype(BF16)
    terms = jnp.dot(hidden, w_down_v[...], preferred_element_type=F32)
    partial[1] = terms.reshape(SIDE, SIDE, OWN, D).astype(BF16)
    mlp_share = reduce_scatter(
        partial.at[1], first_low.at[1], first_high.at[1], mid_low.at[1], mid_high.at[1],
        last_low.at[1], last_high.at[1], y, x, rs_send.at[1], rs_recv.at[1],
    )
    layer_rows = (after_attn + mlp_share).astype(BF16)
    layer_out[0] = layer_rows
    gather_c[y, x] = layer_rows
    gather_first(gather_c, y, x, ag_send.at[2], ag_recv.at[2])
    gather_second(gather_c, y, x, ag_send.at[2], ag_recv.at[2])
    for load in loads[10:]:
        load.wait()
    gather_low(gather_c, ag_recv.at[2])
    low = gather_c.at[:, :, :, LOW]
    send(low, other_c.at[:, :, :, LOW], pair_send.at[0], pair_recv.at[0], {"guide": other})
    gather_high(gather_c, ag_recv.at[2])
    high = gather_c.at[:, :, :, HIGH]
    send(high, other_c.at[:, :, :, HIGH], pair_send.at[1], pair_recv.at[1], {"guide": other})

    def norm_own(at, carry):
        wide = gather_c[pl.ds(at, 1)].astype(F32).reshape(SIDE * OWN, D)
        scaled = wide * norm_factor(wide)
        start = pl.multiple_of(at * SIDE * OWN, SIDE * OWN)
        next_rows[pl.ds(start, SIDE * OWN), :] = (scaled * gains_v[2]).astype(BF16)
        final_rows[guide, pl.ds(start, SIDE * OWN), :] = (scaled * gains_v[3]).astype(BF16)
        return carry

    lax.fori_loop(0, SIDE, norm_own, 0)
    next_qkv[0] = jnp.dot(next_rows[...], w_next_v[...], preferred_element_type=F32).astype(BF16)
    drain(low, pair_recv.at[0])
    drain(high, pair_recv.at[1])

    def norm_other(at, carry):
        wide = other_c[pl.ds(at, 1)].astype(F32).reshape(SIDE * OWN, D)
        start = pl.multiple_of(at * SIDE * OWN, SIDE * OWN)
        final_rows[other, pl.ds(start, SIDE * OWN), :] = rms_norm(wide, gains_v[3]).astype(BF16)
        return carry

    lax.fori_loop(0, SIDE, norm_other, 0)

    request = batch * ROWS + lax.broadcasted_iota(jnp.int32, (ROWS, VOCAB_STEP), 0)
    level = jnp.full((ROWS, VOCAB_STEP), levels[0].astype(F32))
    bound = counts[0]
    for t in range(1, TENANTS):
        level = jnp.where(request >= bound, levels[t].astype(F32), level)
        bound = bound + counts[t]
    weight = level * 0.25

    def score(step, top):
        start = pl.multiple_of(step * VOCAB_STEP, VOCAB_STEP)
        logits = lax.dot_general(
            final_rows[...].reshape(GUIDE * ROWS, D), lm_head_v[pl.ds(start, VOCAB_STEP), :], NT,
            preferred_element_type=F32,
        )
        uncond = logits[ROWS:]
        guided = uncond + weight * (logits[:ROWS] - uncond)
        logprobs[:, pl.ds(start, VOCAB_STEP)] = guided
        return jnp.maximum(top, guided)

    top = lax.fori_loop(
        0, VOCAB_LOCAL // VOCAB_STEP, score, jnp.full((ROWS, VOCAB_STEP), -jnp.inf, F32)
    )
    top = jnp.max(top, axis=1, keepdims=True)

    def add_up(step, total):
        start = pl.multiple_of(step * VOCAB_STEP, VOCAB_STEP)
        return total + jnp.exp(logprobs[:, pl.ds(start, VOCAB_STEP)] - top)

    mass = lax.fori_loop(
        0, VOCAB_LOCAL // VOCAB_STEP, add_up, jnp.zeros((ROWS, VOCAB_STEP), F32)
    )
    mass = jnp.sum(mass, axis=1, keepdims=True)
    column = lax.broadcasted_iota(jnp.int32, (ROWS, ROWS), 1)
    packed = jnp.where(column == 0, top, mass)
    place = guide * TENSOR + me
    mine = jnp.transpose(packed)[0:8]
    stats_own[...] = mine
    stats_all[place] = mine
    for step in range(1, TENSOR):
        there = lax.rem(me + step, TENSOR)
        send(stats_own, stats_all.at[place], a2a_send.at[2], a2a_recv.at[2], {"tensor": there})
    for step in range(TENSOR):
        there = lax.rem(me + step, TENSOR)
        send(
            stats_own, stats_all.at[place], a2a_send.at[2], a2a_recv.at[2],
            {"guide": other, "tensor": there},
        )
    drain(stats_all.at[pl.ds(0, GUIDE * TENSOR - 1)], a2a_recv.at[2])
    peaks = stats_all[:, 0, :]
    peak = jnp.max(peaks, axis=0, keepdims=True)
    total = jnp.sum(stats_all[:, 1, :] * jnp.exp(peaks - peak), axis=0, keepdims=True)
    level = jnp.transpose(jnp.broadcast_to(peak + jnp.log(total), (ROWS, ROWS)))
    level = jnp.concatenate([level] * (VOCAB_STEP // ROWS), axis=1)

    def settle(step, carry):
        start = pl.multiple_of(step * VOCAB_STEP, VOCAB_STEP)
        logprobs[:, pl.ds(start, VOCAB_STEP)] = logprobs[:, pl.ds(start, VOCAB_STEP)] - level
        return carry

    lax.fori_loop(0, VOCAB_LOCAL // VOCAB_STEP, settle, 0)

    for k, buf in enumerate((gather_a, gather_b, gather_c)):
        gather_sent(buf, ag_send.at[k])
    for k in range(2):
        scatter_sent(first_low.at[k], first_high.at[k], last_low.at[k], last_high.at[k], rs_send.at[k])
    drain(request_side.at[pl.ds(0, TENSOR - 1)], a2a_send.at[0])
    drain(head_in.at[pl.ds(0, TENSOR - 1)], a2a_send.at[1])
    drain(stats_all.at[pl.ds(0, GUIDE * TENSOR - 1)], a2a_send.at[2])
    drain(low, pair_send.at[0])
    drain(high, pair_send.at[1])


def local(
    stream, attn_gain, w_qkv, cache_keys, cache_values, cache_len, w_out, mlp_gain, w_gate, w_up, w_down,
    final_gain, lm_head, next_gain, w_next, tenant_counts, guide_level,
):
    hbm = pl.BlockSpec(memory_space=pl.ANY)
    smem = pl.BlockSpec(memory_space=pltpu.SMEM)
    vmem = pl.BlockSpec(memory_space=pltpu.VMEM)
    dma = pltpu.SemaphoreType.DMA
    wide = lambda gain: gain.reshape(1, D)
    return pl.pallas_call(
        kernel,
        name="decode_step",
        out_shape=(
            jax.ShapeDtypeStruct((ROWS, VOCAB_LOCAL), F32),
            jax.ShapeDtypeStruct((1, OWN, D), BF16),
            jax.ShapeDtypeStruct((1, ROWS, QKV_LOCAL), BF16),
        ),
        in_specs=[hbm] * 5 + [smem] + [hbm] * 9 + [smem] * 2,
        out_specs=(vmem, vmem, vmem),
        scratch_shapes=[
            pltpu.VMEM((OWN, D), BF16),
            pltpu.VMEM((4, 1, D), F32),
            pltpu.VMEM((D, QKV_LOCAL), BF16),
            pltpu.VMEM((OWN, SLOTS, KV_WIDTH), BF16),
            pltpu.VMEM((OWN, SLOTS, KV_WIDTH), BF16),
            pltpu.VMEM((ROWS, D), BF16),
            pltpu.VMEM((D, FF_LOCAL), BF16),
            pltpu.VMEM((D, FF_LOCAL), BF16),
            pltpu.VMEM((FF_LOCAL, D), BF16),
            pltpu.VMEM((VOCAB_LOCAL, D), BF16),
            pltpu.VMEM((D, QKV_LOCAL), BF16),
            pltpu.VMEM((SIDE, SIDE, OWN, D), BF16),
            pltpu.VMEM((SIDE, SIDE, OWN, D), BF16),
            pltpu.VMEM((SIDE, SIDE, OWN, D), BF16),
            pltpu.VMEM((SIDE, SIDE, OWN, D), BF16),
            pltpu.VMEM((TENSOR, OWN, QKV_LOCAL), BF16),
            pltpu.VMEM((TENSOR, OWN, QKV_LOCAL), BF16),
            pltpu.VMEM((GROUPS + 2, OWN, KV_WIDTH), F32),
            pltpu.VMEM((GROUPS, OWN, KV_WIDTH), F32),
            pltpu.VMEM((TENSOR, OWN, ROWS), BF16),
            pltpu.VMEM((TENSOR, OWN, ROWS), BF16),
            pltpu.VMEM((2, SIDE, SIDE, OWN, D), BF16),
            pltpu.VMEM((2, SIDE - 1, SIDE, OWN, HALF), BF16),
            pltpu.VMEM((2, SIDE - 1, SIDE, OWN, HALF), BF16),
            pltpu.VMEM((2, SIDE, OWN, HALF), BF16),
            pltpu.VMEM((2, SIDE, OWN, HALF), BF16),
            pltpu.VMEM((2, SIDE - 1, OWN, HALF), BF16),
            pltpu.VMEM((2, SIDE - 1, OWN, HALF), BF16),
            pltpu.VMEM((GUIDE, ROWS, D), BF16),
            pltpu.VMEM((ROWS, D), BF16),
            pltpu.VMEM((8, ROWS), F32),
            pltpu.VMEM((GUIDE * TENSOR, 8, ROWS), F32),
            dma((14,)),
            dma((3, 4)),
            dma((3, 4)),
            dma((2, 4)),
            dma((2, 4)),
            dma((3,)),
            dma((3,)),
            dma((2,)),
            dma((2,)),
        ],
        compiler_params=pltpu.CompilerParams(
            collective_id=0, has_side_effects=True, vmem_limit_bytes=60 * 1024 * 1024
        ),
    )(
        stream, wide(attn_gain), w_qkv, cache_keys, cache_values, cache_len, w_out, wide(mlp_gain),
        w_gate, w_up, w_down, wide(final_gain), lm_head, wide(next_gain), w_next, tenant_counts, guide_level,
    )


def solution(mesh):
    in_specs = (
        P("guide", ("batch", "tensor"), None),
        P(),
        P(None, "tensor"),
        P("guide", ("batch", "tensor"), None, None),
        P("guide", ("batch", "tensor"), None, None),
        P("guide", ("batch", "tensor")),
        P("tensor", None),
        P(),
        P(None, "tensor"),
        P(None, "tensor"),
        P("tensor", None),
        P(),
        P(("guide", "tensor"), None),
        P(),
        P(None, "tensor"),
        P(),
        P(),
    )
    out_specs = (
        P("batch", ("guide", "tensor")),
        P("guide", ("batch", "tensor"), None),
        P("guide", "batch", "tensor"),
    )
    return jax.shard_map(local, mesh=mesh, in_specs=in_specs, out_specs=out_specs, check_vma=False)
```

```python
import functools
import math

import jax
import jax.numpy as jnp
from jax import lax
from jax.experimental import pallas as pl
from jax.experimental.pallas import tpu as pltpu
from jax.sharding import PartitionSpec as P

D = 2048
HEADS = 32
KV_HEADS = 8
GROUPS = HEADS // KV_HEADS
HEAD_DIM = 64
KV_WIDTH = KV_HEADS * HEAD_DIM
TENANTS = 4
SLOTS = 1024
FF_LOCAL = 512
QKV_LOCAL = 192
VOCAB_LOCAL = 2048
ROWS = 128
OWN = 8
SIDE = 4
TENSOR = 16
GUIDE = 2
VOCAB_STEP = 256

EPSILON = 1e-05
ROPE_BASE = 500000.0
MASKED = -1e30
MESH = pl.DeviceIdType.MESH
F32 = jnp.float32
BF16 = jnp.bfloat16
NT = (((1,), (1,)), ((), ()))


def norm_factor(wide):
    return lax.rsqrt(jnp.mean(wide * wide, axis=-1, keepdims=True) + EPSILON)


def rms_norm(wide, gain):
    return wide * norm_factor(wide) * gain


def lane_freq(shape):
    lane = lax.broadcasted_iota(jnp.int32, shape, 1)
    steps_up = (lane % (HEAD_DIM // 2)).astype(F32)
    base_freq = jnp.exp(steps_up * (-2.0 * math.log(ROPE_BASE) / HEAD_DIM))
    wavelen = 2.0 * math.pi / base_freq
    smooth = (8192.0 / wavelen - 1.0) / 3.0
    middle = (1.0 - smooth) * base_freq / 32.0 + smooth * base_freq
    return jnp.where(
        wavelen < 2048.0, base_freq, jnp.where(wavelen > 8192.0, base_freq / 32.0, middle)
    )


def rotate(wide, cosine, sine, first):
    width = wide.shape[-1]
    ahead = pltpu.roll(wide, width - HEAD_DIM // 2, 1)
    behind = pltpu.roll(wide, HEAD_DIM // 2, 1)
    return wide * cosine + jnp.where(first, -ahead, behind) * sine


def spread(block):
    return block.astype(F32).reshape(-1, block.shape[-1]).astype(BF16)


def drain(ref, sem):
    pltpu.make_async_copy(ref, ref, sem).wait()


def send(src, dst, send_sem, recv_sem, device):
    pltpu.make_async_remote_copy(
        src_ref=src,
        dst_ref=dst,
        send_sem=send_sem,
        recv_sem=recv_sem,
        device_id=device,
        device_id_type=MESH,
    ).start()


def distance(step):
    return min(step, SIDE - step)


OFFSETS = sorted(
    ((dy, dx) for dy in range(SIDE) for dx in range(SIDE)),
    key=lambda at: -distance(at[0]) - distance(at[1]),
)


def kernel(
    stream, attn_gain, w_qkv, keys, values, lengths, w_out, mlp_gain, w_gate, w_up, w_down,
    final_gain, lm_head, next_gain, w_next, counts, levels,
    guided_all, level_out, layer_out, next_qkv,
    stream_v, gains_v, w_qkv_v, keys_v, values_v, w_out_v, w_gate_v, w_up_v, w_down_v, lm_head_v, w_next_v,
    stream_all, proj, request_side, queries, mixed, head_out, head_all, w_cols, after_own, after_all, after_rows,
    partial, shares, layer_own, layer_all, layer_other, final_rows, next_rows, stats_own, stats_all,
    load_sems, sends, recvs,
):
    guide = lax.axis_index("guide")
    me = lax.axis_index("tensor")
    batch = lax.axis_index("batch")
    y = me // SIDE
    x = lax.rem(me, SIDE)
    other = 1 - guide
    chips = [lax.rem(y + dy, SIDE) * SIDE + lax.rem(x + dx, SIDE) for dy, dx in OFFSETS]

    barrier = pltpu.get_barrier_semaphore()
    for there in chips:
        pl.semaphore_signal(
            barrier, inc=1, device_id={"guide": other, "tensor": there}, device_id_type=MESH
        )
    for there in chips[:-1]:
        pl.semaphore_signal(barrier, inc=1, device_id={"tensor": there}, device_id_type=MESH)

    loads = [
        pltpu.make_async_copy(stream.at[0], stream_v, load_sems.at[0]),
        pltpu.make_async_copy(attn_gain, gains_v.at[0], load_sems.at[1]),
        pltpu.make_async_copy(w_qkv, w_qkv_v, load_sems.at[2]),
        pltpu.make_async_copy(w_out, w_out_v, load_sems.at[3]),
        pltpu.make_async_copy(keys.at[0], keys_v, load_sems.at[4]),
        pltpu.make_async_copy(values.at[0], values_v, load_sems.at[5]),
        pltpu.make_async_copy(mlp_gain, gains_v.at[1], load_sems.at[6]),
        pltpu.make_async_copy(w_gate, w_gate_v, load_sems.at[7]),
        pltpu.make_async_copy(w_up, w_up_v, load_sems.at[8]),
        pltpu.make_async_copy(w_down, w_down_v, load_sems.at[9]),
        pltpu.make_async_copy(next_gain, gains_v.at[2], load_sems.at[10]),
        pltpu.make_async_copy(final_gain, gains_v.at[3], load_sems.at[11]),
        pltpu.make_async_copy(w_next, w_next_v, load_sems.at[12]),
        pltpu.make_async_copy(lm_head, lm_head_v, load_sems.at[13]),
    ]
    for load in loads:
        load.start()
    left = dict(enumerate(loads))
    finish = []

    def ready(*which):
        for k in which:
            left.pop(k).wait()

    def cross(phase, part, dst, whole):
        for there in chips:
            send(part(there), dst, sends.at[phase], recvs.at[phase], {"guide": other, "tensor": there})
        finish.append(lambda: drain(whole, sends.at[phase]))

    pl.semaphore_wait(barrier, 2 * TENSOR - 1)
    ready(0)
    cross(0, lambda there: stream_v, stream_all.at[me], stream_all)

    row = lax.broadcasted_iota(jnp.int32, (OWN, 2 * HEAD_DIM), 0)
    position = jnp.zeros((OWN, 2 * HEAD_DIM), F32)
    for r in range(OWN):
        position = jnp.where(row == r, lengths[0, r].astype(F32), position)
    angle = position * lane_freq((OWN, 2 * HEAD_DIM))
    cosine = jnp.concatenate([jnp.cos(angle)] * (KV_WIDTH // (2 * HEAD_DIM)), axis=1)
    sine = jnp.concatenate([jnp.sin(angle)] * (KV_WIDTH // (2 * HEAD_DIM)), axis=1)
    ready(1, 2, 3)
    drain(stream_all, recvs.at[0])

    wide = stream_all[...].astype(F32).reshape(ROWS, D)
    rows = rms_norm(wide, gains_v[0]).astype(BF16)
    projected = lax.dot_general(rows, w_qkv_v[...], NT, preferred_element_type=F32)
    proj[:, :, 0:QKV_LOCAL] = projected.reshape(TENSOR, OWN, QKV_LOCAL).astype(BF16)
    cross(1, lambda there: proj.at[there], request_side.at[me], request_side)
    drain(request_side, recvs.at[1])
    cross(
        2,
        lambda there: w_out_v.at[:, pl.ds(pl.multiple_of(there * ROWS, ROWS), ROWS)],
        w_cols.at[me],
        w_cols,
    )

    def piece(column):
        at, j = divmod(column, 3)
        return request_side[at, :, j * HEAD_DIM : (j + 1) * HEAD_DIM].astype(F32)

    lane = lax.broadcasted_iota(jnp.int32, (OWN, KV_WIDTH), 1)
    first = lax.rem(lane, HEAD_DIM) < HEAD_DIM // 2
    for g in range(GROUPS):
        wide = jnp.concatenate([piece(GROUPS * k + g) for k in range(KV_HEADS)], axis=1)
        queries[g] = rotate(wide, cosine, sine, first).astype(BF16).astype(F32) * (HEAD_DIM**-0.5)
    wide = jnp.concatenate([piece(HEADS + k) for k in range(KV_HEADS)], axis=1)
    queries[GROUPS] = rotate(wide, cosine, sine, first).astype(BF16).astype(F32)
    queries[GROUPS + 1] = jnp.concatenate(
        [piece(HEADS + KV_HEADS + k) for k in range(KV_HEADS)], axis=1
    )

    ready(4, 5)
    own_head = lane // HEAD_DIM == lax.broadcasted_iota(jnp.int32, (OWN, KV_WIDTH), 0)
    slot = lax.broadcasted_iota(jnp.int32, (HEADS, SLOTS), 1)

    def attend(r, carry):
        rowed = [
            jnp.where(own_head, jnp.broadcast_to(queries[g, pl.ds(r, 1), :], (KV_HEADS, KV_WIDTH)), 0.0)
            for g in range(GROUPS)
        ]
        spread_q = jnp.concatenate(rowed, axis=0)
        new_key = queries[GROUPS, pl.ds(r, 1), :]
        new_value = queries[GROUPS + 1, pl.ds(r, 1), :]
        scores = lax.dot_general(spread_q.astype(BF16), keys_v[r], NT, preferred_element_type=F32)
        fresh = jnp.sum(spread_q * new_key, axis=1, keepdims=True)
        scores = jnp.where(slot < lengths[0, r], scores, MASKED)
        peak = jnp.maximum(jnp.max(scores, axis=1, keepdims=True), fresh)
        expd = jnp.exp(scores - peak)
        fresh_exp = jnp.exp(fresh - peak)
        total = jnp.sum(expd, axis=1, keepdims=True) + fresh_exp
        weighted = jnp.dot(expd.astype(BF16), values_v[r], preferred_element_type=F32)
        weighted = weighted + fresh_exp.astype(BF16).astype(F32) * new_value
        weighted = weighted / total
        for g in range(GROUPS):
            kept = jnp.where(own_head, weighted[g * KV_HEADS : (g + 1) * KV_HEADS], 0.0)
            mixed[g, pl.ds(r, 1), :] = jnp.sum(kept, axis=0, keepdims=True)
        return carry

    lax.fori_loop(0, OWN, attend, 0, unroll=True)
    for k in range(KV_HEADS):
        here = slice(k * HEAD_DIM, (k + 1) * HEAD_DIM)
        head_out[:, k * GROUPS * HEAD_DIM : (k + 1) * GROUPS * HEAD_DIM] = jnp.concatenate(
            [mixed[g, :, here] for g in range(GROUPS)], axis=1
        ).astype(BF16)
    cross(3, lambda there: head_out, head_all.at[me], head_all)
    drain(w_cols, recvs.at[2])
    drain(head_all, recvs.at[3])

    terms = jnp.dot(
        spread(head_all[...]), w_cols[...].reshape(D, ROWS), preferred_element_type=F32
    )
    wide = stream_all[:, :, pl.ds(pl.multiple_of(me * ROWS, ROWS), ROWS)].astype(F32)
    after_own[...] = (wide + terms.reshape(TENSOR, OWN, ROWS)).astype(BF16)
    cross(4, lambda there: after_own, after_all.at[me], after_all)
    ready(6, 7, 8, 9)
    drain(after_all, recvs.at[4])
    own = after_all.at[:, me]
    send(own, after_rows, sends.at[8], recvs.at[8], {"guide": other})
    finish.append(lambda: drain(after_rows, sends.at[8]))

    wide = jnp.concatenate(
        [after_all[k].astype(F32).reshape(ROWS, ROWS) for k in range(TENSOR)], axis=1
    )
    rows = rms_norm(wide, gains_v[1]).astype(BF16)
    gate = jnp.dot(rows, w_gate_v[...], preferred_element_type=F32)
    upward = jnp.dot(rows, w_up_v[...], preferred_element_type=F32)
    hidden = (gate * jax.nn.sigmoid(gate) * upward).astype(BF16)
    terms = jnp.dot(hidden, w_down_v[...], preferred_element_type=F32)
    partial[...] = terms.reshape(TENSOR, OWN, D).astype(BF16)
    cross(5, lambda there: partial.at[there], shares.at[me], shares)
    drain(after_rows, recvs.at[8])
    wide = jnp.concatenate([after_rows[k].astype(F32) for k in range(TENSOR)], axis=1)
    drain(shares, recvs.at[5])
    share = shares[0].astype(F32)
    for k in range(1, TENSOR):
        share = share + shares[k].astype(F32)
    layer_own[...] = (wide + share).astype(BF16)
    cross(6, lambda there: layer_own, layer_all.at[me], layer_all)

    request = batch * ROWS + lax.broadcasted_iota(jnp.int32, (ROWS, VOCAB_STEP), 0)
    level = jnp.full((ROWS, VOCAB_STEP), levels[0].astype(F32))
    bound = counts[0]
    for t in range(1, TENANTS):
        level = jnp.where(request >= bound, levels[t].astype(F32), level)
        bound = bound + counts[t]
    weight = level * 0.25
    ready(10, 11, 12, 13)
    drain(layer_all, recvs.at[6])
    send(layer_all, layer_other, sends.at[9], recvs.at[9], {"guide": other})
    finish.append(lambda: drain(layer_other, sends.at[9]))
    layer_out[...] = layer_all[me]

    def norm_own(at, carry):
        wide = layer_all[pl.ds(at * SIDE, SIDE)].astype(F32).reshape(SIDE * OWN, D)
        scaled = wide * norm_factor(wide)
        start = pl.multiple_of(at * SIDE * OWN, SIDE * OWN)
        next_rows[pl.ds(start, SIDE * OWN), :] = (scaled * gains_v[2]).astype(BF16)
        final_rows[guide, pl.ds(start, SIDE * OWN), :] = (scaled * gains_v[3]).astype(BF16)
        return carry

    lax.fori_loop(0, SIDE, norm_own, 0)
    drain(layer_other, recvs.at[9])

    def norm_other(at, carry):
        wide = layer_other[pl.ds(at * SIDE, SIDE)].astype(F32).reshape(SIDE * OWN, D)
        start = pl.multiple_of(at * SIDE * OWN, SIDE * OWN)
        final_rows[other, pl.ds(start, SIDE * OWN), :] = rms_norm(wide, gains_v[3]).astype(BF16)
        return carry

    lax.fori_loop(0, SIDE, norm_other, 0)

    def score(step, top):
        start = pl.multiple_of(step * VOCAB_STEP, VOCAB_STEP)
        logits = lax.dot_general(
            final_rows[...].reshape(GUIDE * ROWS, D), lm_head_v[pl.ds(start, VOCAB_STEP), :], NT,
            preferred_element_type=F32,
        )
        uncond = logits[ROWS:]
        guided = uncond + weight * (logits[:ROWS] - uncond)
        guided_all[:, pl.ds(start, VOCAB_STEP)] = guided
        return jnp.maximum(top, guided)

    top = lax.fori_loop(
        0, VOCAB_LOCAL // VOCAB_STEP, score, jnp.full((ROWS, VOCAB_STEP), -jnp.inf, F32)
    )
    top = jnp.max(top, axis=1, keepdims=True)

    def add_up(step, total):
        start = pl.multiple_of(step * VOCAB_STEP, VOCAB_STEP)
        return total + jnp.exp(guided_all[:, pl.ds(start, VOCAB_STEP)] - top)

    mass = lax.fori_loop(
        0, VOCAB_LOCAL // VOCAB_STEP, add_up, jnp.zeros((ROWS, VOCAB_STEP), F32)
    )
    mass = jnp.sum(mass, axis=1, keepdims=True)
    column = lax.broadcasted_iota(jnp.int32, (ROWS, ROWS), 1)
    packed = jnp.where(column == 0, top, mass)
    place = guide * TENSOR + me
    mine = jnp.transpose(packed)[0:8]
    stats_own[...] = mine
    stats_all[place] = mine
    for there in chips:
        send(stats_own, stats_all.at[place], sends.at[7], recvs.at[7], {"guide": other, "tensor": there})
    for there in chips[:-1]:
        send(stats_own, stats_all.at[place], sends.at[7], recvs.at[7], {"tensor": there})
    finish.append(lambda: drain(stats_all.at[pl.ds(0, GUIDE * TENSOR - 1)], sends.at[7]))
    next_qkv[...] = lax.dot_general(
        w_next_v[...], next_rows[...], NT, preferred_element_type=F32
    ).astype(BF16)
    drain(stats_all.at[pl.ds(0, GUIDE * TENSOR - 1)], recvs.at[7])
    peaks = stats_all[:, 0, :]
    peak = jnp.max(peaks, axis=0, keepdims=True)
    total = jnp.sum(stats_all[:, 1, :] * jnp.exp(peaks - peak), axis=0, keepdims=True)
    level_out[...] = jnp.transpose(jnp.broadcast_to(peak + jnp.log(total), (ROWS, ROWS)))

    for last in finish:
        last()


def settle(guided, level, layer_rows, next_rows, logprobs, layer_out, next_qkv):
    layer_out[...] = layer_rows[...]
    next_qkv[...] = next_rows[...]
    wide = jnp.concatenate([level[...]] * (VOCAB_LOCAL // ROWS), axis=1)
    logprobs[...] = guided[...] - wide


def local(
    stream, attn_gain, w_qkv, cache_keys, cache_values, cache_len, w_out, mlp_gain, w_gate, w_up, w_down,
    final_gain, lm_head, next_gain, w_next, tenant_counts, guide_level,
):
    hbm = pl.BlockSpec(memory_space=pl.ANY)
    smem = pl.BlockSpec(memory_space=pltpu.SMEM)
    vmem = pl.BlockSpec(memory_space=pltpu.VMEM)
    dma = pltpu.SemaphoreType.DMA
    wide = lambda gain: gain.reshape(1, D)
    guided, level, layer_rows, next_rows = pl.pallas_call(
        kernel,
        name="decode_step",
        out_shape=(
            jax.ShapeDtypeStruct((ROWS, VOCAB_LOCAL), F32),
            jax.ShapeDtypeStruct((ROWS, ROWS), F32),
            jax.ShapeDtypeStruct((OWN, D), BF16),
            jax.ShapeDtypeStruct((QKV_LOCAL, ROWS), BF16),
        ),
        in_specs=[hbm] * 5 + [smem] + [hbm] * 9 + [smem] * 2,
        out_specs=(vmem, vmem, vmem, vmem),
        scratch_shapes=[
            pltpu.VMEM((OWN, D), BF16),
            pltpu.VMEM((4, 1, D), F32),
            pltpu.VMEM((QKV_LOCAL, D), BF16),
            pltpu.VMEM((OWN, SLOTS, KV_WIDTH), BF16),
            pltpu.VMEM((OWN, SLOTS, KV_WIDTH), BF16),
            pltpu.VMEM((ROWS, D), BF16),
            pltpu.VMEM((D, FF_LOCAL), BF16),
            pltpu.VMEM((D, FF_LOCAL), BF16),
            pltpu.VMEM((FF_LOCAL, D), BF16),
            pltpu.VMEM((VOCAB_LOCAL, D), BF16),
            pltpu.VMEM((QKV_LOCAL, D), BF16),
            pltpu.VMEM((TENSOR, OWN, D), BF16),
            pltpu.VMEM((TENSOR, OWN, QKV_LOCAL), BF16),
            pltpu.VMEM((TENSOR, OWN, QKV_LOCAL), BF16),
            pltpu.VMEM((GROUPS + 2, OWN, KV_WIDTH), F32),
            pltpu.VMEM((GROUPS, OWN, KV_WIDTH), F32),
            pltpu.VMEM((OWN, D), BF16),
            pltpu.VMEM((TENSOR, OWN, D), BF16),
            pltpu.VMEM((TENSOR, ROWS, ROWS), BF16),
            pltpu.VMEM((TENSOR, OWN, ROWS), BF16),
            pltpu.VMEM((TENSOR, TENSOR, OWN, ROWS), BF16),
            pltpu.VMEM((TENSOR, OWN, ROWS), BF16),
            pltpu.VMEM((TENSOR, OWN, D), BF16),
            pltpu.VMEM((TENSOR, OWN, D), BF16),
            pltpu.VMEM((OWN, D), BF16),
            pltpu.VMEM((TENSOR, OWN, D), BF16),
            pltpu.VMEM((TENSOR, OWN, D), BF16),
            pltpu.VMEM((GUIDE, ROWS, D), BF16),
            pltpu.VMEM((ROWS, D), BF16),
            pltpu.VMEM((8, ROWS), F32),
            pltpu.VMEM((GUIDE * TENSOR, 8, ROWS), F32),
            dma((14,)),
            dma((10,)),
            dma((10,)),
        ],
        compiler_params=pltpu.CompilerParams(
            collective_id=0, has_side_effects=True, vmem_limit_bytes=60 * 1024 * 1024
        ),
    )(
        stream, wide(attn_gain), w_qkv.T, cache_keys, cache_values, cache_len, w_out, wide(mlp_gain),
        w_gate, w_up, w_down, wide(final_gain), lm_head, wide(next_gain), w_next.T, tenant_counts, guide_level,
    )

    logprobs, layer_out, next_qkv = pl.pallas_call(
        settle,
        name="settle",
        out_shape=(
            jax.ShapeDtypeStruct((ROWS, VOCAB_LOCAL), F32),
            jax.ShapeDtypeStruct((OWN, D), BF16),
            jax.ShapeDtypeStruct((QKV_LOCAL, ROWS), BF16),
        ),
        in_specs=[vmem] * 4,
        out_specs=(vmem, vmem, vmem),
    )(guided, level, layer_rows, next_rows)
    return logprobs, layer_out[None], next_qkv.T[None]


def solution(mesh):
    in_specs = (
        P("guide", ("batch", "tensor"), None),
        P(),
        P(None, "tensor"),
        P("guide", ("batch", "tensor"), None, None),
        P("guide", ("batch", "tensor"), None, None),
        P("guide", ("batch", "tensor")),
        P("tensor", None),
        P(),
        P(None, "tensor"),
        P(None, "tensor"),
        P("tensor", None),
        P(),
        P(("guide", "tensor"), None),
        P(),
        P(None, "tensor"),
        P(),
        P(),
    )
    out_specs = (
        P("batch", ("guide", "tensor")),
        P("guide", ("batch", "tensor"), None),
        P("guide", "batch", "tensor"),
    )
    return jax.shard_map(local, mesh=mesh, in_specs=in_specs, out_specs=out_specs, check_vma=False)
```

```python
import functools
import math

import jax
import jax.numpy as jnp
from jax import lax
from jax.experimental import pallas as pl
from jax.experimental.pallas import tpu as pltpu
from jax.sharding import PartitionSpec as P

D = 2048
HEADS = 32
KV_HEADS = 8
GROUPS = HEADS // KV_HEADS
HEAD_DIM = 64
KV_WIDTH = KV_HEADS * HEAD_DIM
TENANTS = 4
SLOTS = 1024
FF_LOCAL = 512
QKV_LOCAL = 192
VOCAB_LOCAL = 2048
ROWS = 128
OWN = 8
SIDE = 4
TENSOR = 16
GUIDE = 2
VOCAB_STEP = 256

EPSILON = 1e-05
ROPE_BASE = 500000.0
MASKED = -1e30
MESH = pl.DeviceIdType.MESH
F32 = jnp.float32
BF16 = jnp.bfloat16
NT = (((1,), (1,)), ((), ()))


def norm_factor(wide):
    return lax.rsqrt(jnp.mean(wide * wide, axis=-1, keepdims=True) + EPSILON)


def rms_norm(wide, gain):
    return wide * norm_factor(wide) * gain


def lane_freq(shape):
    lane = lax.broadcasted_iota(jnp.int32, shape, 1)
    steps_up = (lane % (HEAD_DIM // 2)).astype(F32)
    base_freq = jnp.exp(steps_up * (-2.0 * math.log(ROPE_BASE) / HEAD_DIM))
    wavelen = 2.0 * math.pi / base_freq
    smooth = (8192.0 / wavelen - 1.0) / 3.0
    middle = (1.0 - smooth) * base_freq / 32.0 + smooth * base_freq
    return jnp.where(
        wavelen < 2048.0, base_freq, jnp.where(wavelen > 8192.0, base_freq / 32.0, middle)
    )


def rotate(wide, cosine, sine, first):
    width = wide.shape[-1]
    ahead = pltpu.roll(wide, width - HEAD_DIM // 2, 1)
    behind = pltpu.roll(wide, HEAD_DIM // 2, 1)
    return wide * cosine + jnp.where(first, -ahead, behind) * sine


def spread(block):
    return block.astype(F32).reshape(-1, block.shape[-1]).astype(BF16)


def drain(ref, sem):
    pltpu.make_async_copy(ref, ref, sem).wait()


def send(src, dst, send_sem, recv_sem, device):
    pltpu.make_async_remote_copy(
        src_ref=src,
        dst_ref=dst,
        send_sem=send_sem,
        recv_sem=recv_sem,
        device_id=device,
        device_id_type=MESH,
    ).start()


def distance(step):
    return min(step, SIDE - step)


OFFSETS = sorted(
    ((dy, dx) for dy in range(SIDE) for dx in range(SIDE)),
    key=lambda at: -distance(at[0]) - distance(at[1]),
)


def kernel(
    stream, attn_gain, w_qkv, keys, values, lengths, w_out, mlp_gain, w_gate, w_up, w_down,
    final_gain, lm_head, next_gain, w_next, counts, levels,
    guided_all, level_out, layer_out, next_qkv,
    stream_v, gains_v, w_qkv_v, keys_v, values_v, w_out_v, w_gate_v, w_up_v, w_down_v, lm_head_v, w_next_v,
    stream_all, proj, request_side, queries, scores, probs, mixed, head_out, head_all, w_cols, after_own, after_all, after_rows,
    partial, shares, layer_own, layer_all, final_rows, cond_all, stats_own, stats_all,
    load_sems, sends, recvs,
):
    guide = lax.axis_index("guide")
    me = lax.axis_index("tensor")
    batch = lax.axis_index("batch")
    y = me // SIDE
    x = lax.rem(me, SIDE)
    other = 1 - guide
    chips = [lax.rem(y + dy, SIDE) * SIDE + lax.rem(x + dx, SIDE) for dy, dx in OFFSETS]

    barrier = pltpu.get_barrier_semaphore()
    for there in chips:
        pl.semaphore_signal(
            barrier, inc=1, device_id={"guide": other, "tensor": there}, device_id_type=MESH
        )
    for there in chips[:-1]:
        pl.semaphore_signal(barrier, inc=1, device_id={"tensor": there}, device_id_type=MESH)

    loads = [
        pltpu.make_async_copy(stream.at[0], stream_v, load_sems.at[0]),
        pltpu.make_async_copy(attn_gain, gains_v.at[0], load_sems.at[1]),
        pltpu.make_async_copy(w_qkv, w_qkv_v, load_sems.at[2]),
        pltpu.make_async_copy(w_out, w_out_v, load_sems.at[3]),
        pltpu.make_async_copy(keys.at[0], keys_v, load_sems.at[4]),
        pltpu.make_async_copy(values.at[0], values_v, load_sems.at[5]),
        pltpu.make_async_copy(mlp_gain, gains_v.at[1], load_sems.at[6]),
        pltpu.make_async_copy(w_gate, w_gate_v, load_sems.at[7]),
        pltpu.make_async_copy(w_up, w_up_v, load_sems.at[8]),
        pltpu.make_async_copy(w_down, w_down_v, load_sems.at[9]),
        pltpu.make_async_copy(next_gain, gains_v.at[2], load_sems.at[10]),
        pltpu.make_async_copy(final_gain, gains_v.at[3], load_sems.at[11]),
        pltpu.make_async_copy(w_next, w_next_v, load_sems.at[12]),
        pltpu.make_async_copy(lm_head, lm_head_v, load_sems.at[13]),
    ]
    for load in loads:
        load.start()
    left = dict(enumerate(loads))
    finish = []

    def ready(*which):
        for k in which:
            left.pop(k).wait()

    def cross(phase, part, dst, whole, early=None):
        for offset, there in zip(OFFSETS, chips):
            landed = recvs.at[10] if offset == early else recvs.at[phase]
            send(part(there), dst, sends.at[phase], landed, {"guide": other, "tensor": there})
        finish.append(lambda: drain(whole, sends.at[phase]))

    pl.semaphore_wait(barrier, 2 * TENSOR - 1)
    ready(0)
    pl.when(guide == 1)(lambda: drain(stream_all.at[0], recvs.at[10]))
    cross(0, lambda there: stream_v, stream_all.at[me], stream_all, early=(0, 1))
    pl.when(guide == 0)(lambda: drain(stream_all.at[0], recvs.at[10]))

    row = lax.broadcasted_iota(jnp.int32, (OWN, 2 * HEAD_DIM), 0)
    position = jnp.zeros((OWN, 2 * HEAD_DIM), F32)
    for r in range(OWN):
        position = jnp.where(row == r, lengths[0, r].astype(F32), position)
    angle = position * lane_freq((OWN, 2 * HEAD_DIM))
    cosine = jnp.concatenate([jnp.cos(angle)] * (KV_WIDTH // (2 * HEAD_DIM)), axis=1)
    sine = jnp.concatenate([jnp.sin(angle)] * (KV_WIDTH // (2 * HEAD_DIM)), axis=1)
    ready(1, 2, 3)
    drain(stream_all.at[pl.ds(0, TENSOR - 1)], recvs.at[0])

    wide = stream_all[...].astype(F32).reshape(ROWS, D)
    rows = rms_norm(wide, gains_v[0]).astype(BF16)
    projected = lax.dot_general(rows, w_qkv_v[...], NT, preferred_element_type=F32)
    proj[:, :, 0:QKV_LOCAL] = projected.reshape(TENSOR, OWN, QKV_LOCAL).astype(BF16)
    cross(1, lambda there: proj.at[there], request_side.at[me], request_side)
    half = pl.ds(pl.multiple_of(guide * (ROWS // 2), ROWS // 2), ROWS // 2)
    rest = pl.ds(pl.multiple_of(other * (ROWS // 2), ROWS // 2), ROWS // 2)
    cross(
        2,
        lambda there: w_out_v.at[half, pl.ds(pl.multiple_of(there * ROWS, ROWS), ROWS)],
        w_cols.at[me, half],
        w_cols.at[:, half],
    )
    drain(request_side, recvs.at[1])

    def piece(column):
        at, j = divmod(column, 3)
        return request_side[at, :, j * HEAD_DIM : (j + 1) * HEAD_DIM].astype(F32)

    lane = lax.broadcasted_iota(jnp.int32, (OWN, KV_WIDTH), 1)
    first = lax.rem(lane, HEAD_DIM) < HEAD_DIM // 2
    for g in range(GROUPS):
        wide = jnp.concatenate([piece(GROUPS * k + g) for k in range(KV_HEADS)], axis=1)
        queries[g] = rotate(wide, cosine, sine, first).astype(BF16).astype(F32) * (HEAD_DIM**-0.5)
    wide = jnp.concatenate([piece(HEADS + k) for k in range(KV_HEADS)], axis=1)
    queries[GROUPS] = rotate(wide, cosine, sine, first).astype(BF16).astype(F32)
    queries[GROUPS + 1] = jnp.concatenate(
        [piece(HEADS + KV_HEADS + k) for k in range(KV_HEADS)], axis=1
    )

    ready(4, 5)
    own_head = lane // HEAD_DIM == lax.broadcasted_iota(jnp.int32, (OWN, KV_WIDTH), 0)
    slot = lax.broadcasted_iota(jnp.int32, (HEADS, SLOTS), 1)

    fresh = []
    for r in range(OWN):
        spread_q = jnp.concatenate(
            [
                jnp.where(own_head, jnp.broadcast_to(queries[g, r : r + 1, :], (KV_HEADS, KV_WIDTH)), 0.0)
                for g in range(GROUPS)
            ],
            axis=0,
        )
        scores[r] = lax.dot_general(spread_q.astype(BF16), keys_v[r], NT, preferred_element_type=F32)
        fresh.append(jnp.sum(spread_q * queries[GROUPS, r : r + 1, :], axis=1, keepdims=True))
    drain(w_cols.at[:, rest], recvs.at[2])
    send(w_cols.at[:, rest], w_cols.at[:, rest], sends.at[11], recvs.at[11], {"guide": other})
    finish.append(lambda: drain(w_cols.at[:, rest], sends.at[11]))
    totals = []
    for r in range(OWN):
        masked = jnp.where(slot < lengths[0, r], scores[r], MASKED)
        peak = jnp.maximum(jnp.max(masked, axis=1, keepdims=True), fresh[r])
        expd = jnp.exp(masked - peak)
        fresh[r] = jnp.exp(fresh[r] - peak)
        totals.append(jnp.sum(expd, axis=1, keepdims=True) + fresh[r])
        probs[r] = expd.astype(BF16)
    for r in range(OWN):
        weighted = jnp.dot(probs[r], values_v[r], preferred_element_type=F32)
        weighted = weighted + fresh[r].astype(BF16).astype(F32) * queries[GROUPS + 1, r : r + 1, :]
        weighted = weighted / totals[r]
        for g in range(GROUPS):
            kept = jnp.where(own_head, weighted[g * KV_HEADS : (g + 1) * KV_HEADS], 0.0)
            mixed[g, r : r + 1, :] = jnp.sum(kept, axis=0, keepdims=True)
    for k in range(KV_HEADS):
        here = slice(k * HEAD_DIM, (k + 1) * HEAD_DIM)
        head_out[:, k * GROUPS * HEAD_DIM : (k + 1) * GROUPS * HEAD_DIM] = jnp.concatenate(
            [mixed[g, :, here] for g in range(GROUPS)], axis=1
        ).astype(BF16)
    cross(3, lambda there: head_out, head_all.at[me], head_all)
    drain(w_cols.at[:, half], recvs.at[11])
    drain(head_all, recvs.at[3])

    terms = jnp.dot(
        spread(head_all[...]), w_cols[...].reshape(D, ROWS), preferred_element_type=F32
    )
    wide = stream_all[:, :, pl.ds(pl.multiple_of(me * ROWS, ROWS), ROWS)].astype(F32)
    after_own[...] = (wide + terms.reshape(TENSOR, OWN, ROWS)).astype(BF16)
    cross(4, lambda there: after_own, after_all.at[me], after_all)
    ready(6, 7, 8, 9)
    drain(after_all, recvs.at[4])
    own = after_all.at[:, me]
    send(own, after_rows, sends.at[8], recvs.at[8], {"guide": other})
    finish.append(lambda: drain(after_rows, sends.at[8]))

    wide = jnp.concatenate(
        [after_all[k].astype(F32).reshape(ROWS, ROWS) for k in range(TENSOR)], axis=1
    )
    rows = rms_norm(wide, gains_v[1]).astype(BF16)
    gate = jnp.dot(rows, w_gate_v[...], preferred_element_type=F32)
    upward = jnp.dot(rows, w_up_v[...], preferred_element_type=F32)
    hidden = (gate * jax.nn.sigmoid(gate) * upward).astype(BF16)
    terms = jnp.dot(hidden, w_down_v[...], preferred_element_type=F32)
    partial[...] = terms.reshape(TENSOR, OWN, D).astype(BF16)
    cross(5, lambda there: partial.at[there], shares.at[me], shares)
    drain(after_rows, recvs.at[8])
    wide = jnp.concatenate([after_rows[k].astype(F32) for k in range(TENSOR)], axis=1)
    drain(shares, recvs.at[5])
    share = shares[0].astype(F32)
    for k in range(1, TENSOR):
        share = share + shares[k].astype(F32)
    layer_own[...] = (wide + share).astype(BF16)
    cross(6, lambda there: layer_own, layer_all.at[other, me], layer_all.at[other])

    request = batch * ROWS + lax.broadcasted_iota(jnp.int32, (ROWS, VOCAB_STEP), 0)
    level = jnp.full((ROWS, VOCAB_STEP), levels[0].astype(F32))
    bound = counts[0]
    for t in range(1, TENANTS):
        level = jnp.where(request >= bound, levels[t].astype(F32), level)
        bound = bound + counts[t]
    weight = level * 0.25
    ready(10, 11, 12, 13)

    def arrive(branch):
        @pl.when(guide == branch)
        def _():
            drain(layer_all.at[branch], recvs.at[6])
            send(layer_all.at[branch], layer_all.at[branch], sends.at[9], recvs.at[9], {"guide": other})

        pl.when(guide != branch)(lambda: drain(layer_all.at[branch], recvs.at[9]))
        for at in range(0, TENSOR, SIDE):
            wide = layer_all[branch, at : at + SIDE].astype(F32).reshape(SIDE * OWN, D)
            final_rows[at * OWN : (at + SIDE) * OWN] = rms_norm(wide, gains_v[3]).astype(BF16)

    def logits(step):
        return lax.dot_general(
            final_rows[...], lm_head_v[step * VOCAB_STEP : (step + 1) * VOCAB_STEP], NT,
            preferred_element_type=F32,
        )

    steps = VOCAB_LOCAL // VOCAB_STEP
    arrive(0)
    for step in range(steps):
        cond_all[:, step * VOCAB_STEP : (step + 1) * VOCAB_STEP] = logits(step)
    arrive(1)
    finish.append(lambda: drain(layer_all.at[0], sends.at[9]))
    top = jnp.full((ROWS, VOCAB_STEP), -jnp.inf, F32)
    for step in range(steps):
        here = slice(step * VOCAB_STEP, (step + 1) * VOCAB_STEP)
        uncond = logits(step)
        guided = uncond + weight * (cond_all[:, here] - uncond)
        cond_all[:, here] = guided
        top = jnp.maximum(top, guided)
        copy = pltpu.make_async_copy(cond_all.at[:, here], guided_all.at[:, here], load_sems.at[step])
        copy.start()
        finish.append(copy.wait)
    top = jnp.max(top, axis=1, keepdims=True)
    mass = jnp.zeros((ROWS, VOCAB_STEP), F32)
    for step in range(steps):
        mass = mass + jnp.exp(cond_all[:, step * VOCAB_STEP : (step + 1) * VOCAB_STEP] - top)
    mass = jnp.sum(mass, axis=1, keepdims=True)
    column = lax.broadcasted_iota(jnp.int32, (ROWS, ROWS), 1)
    packed = jnp.where(column == 0, top, mass)
    place = guide * TENSOR + me
    mine = jnp.transpose(packed)[0:8]
    stats_own[...] = mine
    stats_all[place] = mine
    for there in chips:
        send(stats_own, stats_all.at[place], sends.at[7], recvs.at[7], {"guide": other, "tensor": there})
    for there in chips[:-1]:
        send(stats_own, stats_all.at[place], sends.at[7], recvs.at[7], {"tensor": there})
    finish.append(lambda: drain(stats_all.at[pl.ds(0, GUIDE * TENSOR - 1)], sends.at[7]))

    layer_out[...] = layer_all[guide, me]
    for at in range(0, TENSOR, SIDE):
        wide = layer_all[guide, pl.ds(at, SIDE)].astype(F32).reshape(SIDE * OWN, D)
        final_rows[at * OWN : (at + SIDE) * OWN] = rms_norm(wide, gains_v[2]).astype(BF16)
    next_qkv[...] = lax.dot_general(
        w_next_v[...], final_rows[...], NT, preferred_element_type=F32
    ).astype(BF16)
    drain(stats_all.at[pl.ds(0, GUIDE * TENSOR - 1)], recvs.at[7])
    peaks = stats_all[:, 0, :]
    peak = jnp.max(peaks, axis=0, keepdims=True)
    total = jnp.sum(stats_all[:, 1, :] * jnp.exp(peaks - peak), axis=0, keepdims=True)
    level_out[...] = jnp.transpose(jnp.broadcast_to(peak + jnp.log(total), (ROWS, ROWS)))

    for last in finish:
        last()


def settle(guided, level, layer_rows, next_rows, logprobs, layer_out, next_qkv):
    layer_out[...] = layer_rows[...]
    next_qkv[...] = next_rows[...]
    wide = jnp.concatenate([level[...]] * (VOCAB_LOCAL // ROWS), axis=1)
    logprobs[...] = guided[...] - wide


def local(
    stream, attn_gain, w_qkv, cache_keys, cache_values, cache_len, w_out, mlp_gain, w_gate, w_up, w_down,
    final_gain, lm_head, next_gain, w_next, tenant_counts, guide_level,
):
    hbm = pl.BlockSpec(memory_space=pl.ANY)
    smem = pl.BlockSpec(memory_space=pltpu.SMEM)
    vmem = pl.BlockSpec(memory_space=pltpu.VMEM)
    dma = pltpu.SemaphoreType.DMA
    wide = lambda gain: gain.reshape(1, D)
    guided, level, layer_rows, next_rows = pl.pallas_call(
        kernel,
        name="decode_step",
        out_shape=(
            jax.ShapeDtypeStruct((ROWS, VOCAB_LOCAL), F32),
            jax.ShapeDtypeStruct((ROWS, ROWS), F32),
            jax.ShapeDtypeStruct((OWN, D), BF16),
            jax.ShapeDtypeStruct((QKV_LOCAL, ROWS), BF16),
        ),
        in_specs=[hbm] * 5 + [smem] + [hbm] * 9 + [smem] * 2,
        out_specs=(hbm, vmem, vmem, vmem),
        scratch_shapes=[
            pltpu.VMEM((OWN, D), BF16),
            pltpu.VMEM((4, 1, D), F32),
            pltpu.VMEM((QKV_LOCAL, D), BF16),
            pltpu.VMEM((OWN, SLOTS, KV_WIDTH), BF16),
            pltpu.VMEM((OWN, SLOTS, KV_WIDTH), BF16),
            pltpu.VMEM((ROWS, D), BF16),
            pltpu.VMEM((D, FF_LOCAL), BF16),
            pltpu.VMEM((D, FF_LOCAL), BF16),
            pltpu.VMEM((FF_LOCAL, D), BF16),
            pltpu.VMEM((VOCAB_LOCAL, D), BF16),
            pltpu.VMEM((QKV_LOCAL, D), BF16),
            pltpu.VMEM((TENSOR, OWN, D), BF16),
            pltpu.VMEM((TENSOR, OWN, QKV_LOCAL), BF16),
            pltpu.VMEM((TENSOR, OWN, QKV_LOCAL), BF16),
            pltpu.VMEM((GROUPS + 2, OWN, KV_WIDTH), F32),
            pltpu.VMEM((OWN, HEADS, SLOTS), F32),
            pltpu.VMEM((OWN, HEADS, SLOTS), BF16),
            pltpu.VMEM((GROUPS, OWN, KV_WIDTH), F32),
            pltpu.VMEM((OWN, D), BF16),
            pltpu.VMEM((TENSOR, OWN, D), BF16),
            pltpu.VMEM((TENSOR, ROWS, ROWS), BF16),
            pltpu.VMEM((TENSOR, OWN, ROWS), BF16),
            pltpu.VMEM((TENSOR, TENSOR, OWN, ROWS), BF16),
            pltpu.VMEM((TENSOR, OWN, ROWS), BF16),
            pltpu.VMEM((TENSOR, OWN, D), BF16),
            pltpu.VMEM((TENSOR, OWN, D), BF16),
            pltpu.VMEM((OWN, D), BF16),
            pltpu.VMEM((GUIDE, TENSOR, OWN, D), BF16),
            pltpu.VMEM((ROWS, D), BF16),
            pltpu.VMEM((ROWS, VOCAB_LOCAL), F32),
            pltpu.VMEM((8, ROWS), F32),
            pltpu.VMEM((GUIDE * TENSOR, 8, ROWS), F32),
            dma((14,)),
            dma((12,)),
            dma((12,)),
        ],
        compiler_params=pltpu.CompilerParams(
            collective_id=0, has_side_effects=True, vmem_limit_bytes=60 * 1024 * 1024
        ),
    )(
        stream, wide(attn_gain), w_qkv.T, cache_keys, cache_values, cache_len, w_out, wide(mlp_gain),
        w_gate, w_up, w_down, wide(final_gain), lm_head, wide(next_gain), w_next.T, tenant_counts, guide_level,
    )

    logprobs, layer_out, next_qkv = pl.pallas_call(
        settle,
        name="settle",
        out_shape=(
            jax.ShapeDtypeStruct((ROWS, VOCAB_LOCAL), F32),
            jax.ShapeDtypeStruct((OWN, D), BF16),
            jax.ShapeDtypeStruct((QKV_LOCAL, ROWS), BF16),
        ),
        in_specs=[vmem] * 4,
        out_specs=(vmem, vmem, vmem),
    )(guided, level, layer_rows, next_rows)
    return logprobs, layer_out[None], next_qkv.T[None]


def solution(mesh):
    in_specs = (
        P("guide", ("batch", "tensor"), None),
        P(),
        P(None, "tensor"),
        P("guide", ("batch", "tensor"), None, None),
        P("guide", ("batch", "tensor"), None, None),
        P("guide", ("batch", "tensor")),
        P("tensor", None),
        P(),
        P(None, "tensor"),
        P(None, "tensor"),
        P("tensor", None),
        P(),
        P(("guide", "tensor"), None),
        P(),
        P(None, "tensor"),
        P(),
        P(),
    )
    out_specs = (
        P("batch", ("guide", "tensor")),
        P("guide", ("batch", "tensor"), None),
        P("guide", "batch", "tensor"),
    )
    return jax.shard_map(local, mesh=mesh, in_specs=in_specs, out_specs=out_specs, check_vma=False)
```

```python
import functools
import math

import jax
import jax.numpy as jnp
from jax import lax
from jax.experimental import pallas as pl
from jax.experimental.pallas import tpu as pltpu
from jax.sharding import PartitionSpec as P

D = 2048
HEADS = 32
KV_HEADS = 8
GROUPS = HEADS // KV_HEADS
HEAD_DIM = 64
KV_WIDTH = KV_HEADS * HEAD_DIM
TENANTS = 4
SLOTS = 1024
FF_LOCAL = 512
QKV_LOCAL = 192
VOCAB_LOCAL = 2048
ROWS = 128
OWN = 8
SIDE = 4
TENSOR = 16
GUIDE = 2
VOCAB_STEP = 256

EPSILON = 1e-05
ROPE_BASE = 500000.0
MASKED = -1e30
MESH = pl.DeviceIdType.MESH
F32 = jnp.float32
BF16 = jnp.bfloat16
NT = (((1,), (1,)), ((), ()))


def norm_factor(wide):
    return lax.rsqrt(jnp.mean(wide * wide, axis=-1, keepdims=True) + EPSILON)


def rms_norm(wide, gain):
    return wide * norm_factor(wide) * gain


def lane_freq(shape):
    lane = lax.broadcasted_iota(jnp.int32, shape, 1)
    steps_up = (lane % (HEAD_DIM // 2)).astype(F32)
    base_freq = jnp.exp(steps_up * (-2.0 * math.log(ROPE_BASE) / HEAD_DIM))
    wavelen = 2.0 * math.pi / base_freq
    smooth = (8192.0 / wavelen - 1.0) / 3.0
    middle = (1.0 - smooth) * base_freq / 32.0 + smooth * base_freq
    return jnp.where(
        wavelen < 2048.0, base_freq, jnp.where(wavelen > 8192.0, base_freq / 32.0, middle)
    )


def rotate(wide, cosine, sine, first):
    width = wide.shape[-1]
    ahead = pltpu.roll(wide, width - HEAD_DIM // 2, 1)
    behind = pltpu.roll(wide, HEAD_DIM // 2, 1)
    return wide * cosine + jnp.where(first, -ahead, behind) * sine


def spread(block):
    return block.astype(F32).reshape(-1, block.shape[-1]).astype(BF16)


def drain(ref, sem):
    pltpu.make_async_copy(ref, ref, sem).wait()


def send(src, dst, send_sem, recv_sem, device):
    pltpu.make_async_remote_copy(
        src_ref=src,
        dst_ref=dst,
        send_sem=send_sem,
        recv_sem=recv_sem,
        device_id=device,
        device_id_type=MESH,
    ).start()


OFFSETS = (
    (2, 2), (1, 2), (2, 1), (3, 2), (2, 3), (1, 1), (3, 3), (1, 3), (3, 1),
    (0, 2), (2, 0), (0, 1), (1, 0), (0, 3), (3, 0), (0, 0),
)


def kernel(
    stream, attn_gain, w_qkv, keys, values, lengths, w_out, mlp_gain, w_gate, w_up, w_down,
    final_gain, lm_head, next_gain, w_next, counts, levels,
    guided_all, level_out, layer_out, next_qkv,
    stream_v, gains_v, w_qkv_v, keys_v, values_v, w_out_v, w_gate_v, w_up_v, w_down_v, lm_head_v, w_next_v,
    lm_head_t, stream_all, proj, request_side, queries, scores, probs, mixed, head_out, head_all, w_cols, after_own, after_all, after_rows,
    partial, shares, layer_own, layer_all, final_rows, cond_all, next_own, stats_own, stats_all,
    load_sems, sends, recvs,
):
    guide = lax.axis_index("guide")
    me = lax.axis_index("tensor")
    batch = lax.axis_index("batch")
    y = me // SIDE
    x = lax.rem(me, SIDE)
    other = 1 - guide
    chips = [lax.rem(y + dy, SIDE) * SIDE + lax.rem(x + dx, SIDE) for dy, dx in OFFSETS]

    barrier = pltpu.get_barrier_semaphore()
    for there in chips:
        pl.semaphore_signal(
            barrier, inc=1, device_id={"guide": other, "tensor": there}, device_id_type=MESH
        )
    for there in chips[:-1]:
        pl.semaphore_signal(barrier, inc=1, device_id={"tensor": there}, device_id_type=MESH)

    loads = [
        pltpu.make_async_copy(stream.at[0], stream_v, load_sems.at[0]),
        pltpu.make_async_copy(attn_gain, gains_v.at[0], load_sems.at[1]),
        pltpu.make_async_copy(w_qkv, w_qkv_v, load_sems.at[2]),
        pltpu.make_async_copy(w_out, w_out_v, load_sems.at[3]),
        pltpu.make_async_copy(keys.at[0], keys_v, load_sems.at[4]),
        pltpu.make_async_copy(values.at[0], values_v, load_sems.at[5]),
        pltpu.make_async_copy(mlp_gain, gains_v.at[1], load_sems.at[6]),
        pltpu.make_async_copy(w_gate, w_gate_v, load_sems.at[7]),
        pltpu.make_async_copy(w_up, w_up_v, load_sems.at[8]),
        pltpu.make_async_copy(w_down, w_down_v, load_sems.at[9]),
        pltpu.make_async_copy(next_gain, gains_v.at[2], load_sems.at[10]),
        pltpu.make_async_copy(final_gain, gains_v.at[3], load_sems.at[11]),
        pltpu.make_async_copy(w_next, w_next_v, load_sems.at[12]),
        pltpu.make_async_copy(lm_head, lm_head_v, load_sems.at[13]),
    ]
    for load in loads:
        load.start()
    left = dict(enumerate(loads))
    finish = []

    def ready(*which):
        for k in which:
            left.pop(k).wait()

    def cross(phase, part, dst, whole, early=None):
        for offset, there in zip(OFFSETS, chips):
            landed = recvs.at[10] if offset == early else recvs.at[phase]
            send(part(there), dst, sends.at[phase], landed, {"guide": other, "tensor": there})
        finish.append(lambda: drain(whole, sends.at[phase]))

    pl.semaphore_wait(barrier, 2 * TENSOR - 1)
    ready(0)
    pl.when(guide == 1)(lambda: drain(stream_all.at[0], recvs.at[10]))
    cross(0, lambda there: stream_v, stream_all.at[me], stream_all, early=(0, 1))
    pl.when(guide == 0)(lambda: drain(stream_all.at[0], recvs.at[10]))

    row = lax.broadcasted_iota(jnp.int32, (OWN, 2 * HEAD_DIM), 0)
    position = jnp.zeros((OWN, 2 * HEAD_DIM), F32)
    for r in range(OWN):
        position = jnp.where(row == r, lengths[0, r].astype(F32), position)
    angle = position * lane_freq((OWN, 2 * HEAD_DIM))
    cosine = jnp.concatenate([jnp.cos(angle)] * (KV_WIDTH // (2 * HEAD_DIM)), axis=1)
    sine = jnp.concatenate([jnp.sin(angle)] * (KV_WIDTH // (2 * HEAD_DIM)), axis=1)
    ready(1, 2, 3)
    drain(stream_all.at[pl.ds(0, TENSOR - 1)], recvs.at[0])

    wide = stream_all[...].astype(F32).reshape(ROWS, D)
    rows = rms_norm(wide, gains_v[0]).astype(BF16)
    projected = lax.dot_general(rows, w_qkv_v[...], NT, preferred_element_type=F32)
    proj[:, :, 0:QKV_LOCAL] = projected.reshape(TENSOR, OWN, QKV_LOCAL).astype(BF16)
    cross(1, lambda there: proj.at[there], request_side.at[me], request_side)
    half = pl.ds(pl.multiple_of(guide * (ROWS // 2), ROWS // 2), ROWS // 2)
    rest = pl.ds(pl.multiple_of(other * (ROWS // 2), ROWS // 2), ROWS // 2)
    cross(
        2,
        lambda there: w_out_v.at[half, pl.ds(pl.multiple_of(there * ROWS, ROWS), ROWS)],
        w_cols.at[me, half],
        w_cols.at[:, half],
    )
    drain(request_side, recvs.at[1])

    def piece(column):
        at, j = divmod(column, 3)
        return request_side[at, :, j * HEAD_DIM : (j + 1) * HEAD_DIM].astype(F32)

    lane = lax.broadcasted_iota(jnp.int32, (OWN, KV_WIDTH), 1)
    first = lax.rem(lane, HEAD_DIM) < HEAD_DIM // 2
    for g in range(GROUPS):
        wide = jnp.concatenate([piece(GROUPS * k + g) for k in range(KV_HEADS)], axis=1)
        queries[g] = rotate(wide, cosine, sine, first).astype(BF16).astype(F32) * (HEAD_DIM**-0.5)
    wide = jnp.concatenate([piece(HEADS + k) for k in range(KV_HEADS)], axis=1)
    queries[GROUPS] = rotate(wide, cosine, sine, first).astype(BF16).astype(F32)
    queries[GROUPS + 1] = jnp.concatenate(
        [piece(HEADS + KV_HEADS + k) for k in range(KV_HEADS)], axis=1
    )

    ready(4, 5)
    own_head = lane // HEAD_DIM == lax.broadcasted_iota(jnp.int32, (OWN, KV_WIDTH), 0)
    slot = lax.broadcasted_iota(jnp.int32, (HEADS, SLOTS), 1)

    fresh = []
    for r in range(OWN):
        spread_q = jnp.concatenate(
            [
                jnp.where(own_head, jnp.broadcast_to(queries[g, r : r + 1, :], (KV_HEADS, KV_WIDTH)), 0.0)
                for g in range(GROUPS)
            ],
            axis=0,
        )
        scores[r] = lax.dot_general(spread_q.astype(BF16), keys_v[r], NT, preferred_element_type=F32)
        fresh.append(jnp.sum(spread_q * queries[GROUPS, r : r + 1, :], axis=1, keepdims=True))
    drain(w_cols.at[:, rest], recvs.at[2])
    send(w_cols.at[:, rest], w_cols.at[:, rest], sends.at[11], recvs.at[11], {"guide": other})
    finish.append(lambda: drain(w_cols.at[:, rest], sends.at[11]))
    totals = []
    for r in range(OWN):
        masked = jnp.where(slot < lengths[0, r], scores[r], MASKED)
        peak = jnp.maximum(jnp.max(masked, axis=1, keepdims=True), fresh[r])
        expd = jnp.exp(masked - peak)
        fresh[r] = jnp.exp(fresh[r] - peak)
        totals.append(jnp.sum(expd, axis=1, keepdims=True) + fresh[r])
        probs[r] = expd.astype(BF16)
    for r in range(OWN):
        weighted = jnp.dot(probs[r], values_v[r], preferred_element_type=F32)
        weighted = weighted + fresh[r].astype(BF16).astype(F32) * queries[GROUPS + 1, r : r + 1, :]
        weighted = weighted / totals[r]
        for g in range(GROUPS):
            kept = jnp.where(own_head, weighted[g * KV_HEADS : (g + 1) * KV_HEADS], 0.0)
            mixed[g, r : r + 1, :] = jnp.sum(kept, axis=0, keepdims=True)
    for k in range(KV_HEADS):
        here = slice(k * HEAD_DIM, (k + 1) * HEAD_DIM)
        head_out[:, k * GROUPS * HEAD_DIM : (k + 1) * GROUPS * HEAD_DIM] = jnp.concatenate(
            [mixed[g, :, here] for g in range(GROUPS)], axis=1
        ).astype(BF16)
    cross(3, lambda there: head_out, head_all.at[me], head_all)
    ready(13)

    def turn_head(step, carry):
        here = pl.ds(pl.multiple_of(step * VOCAB_STEP, VOCAB_STEP), VOCAB_STEP)
        lm_head_t[:, here] = lm_head_v[here, :].T
        return carry

    lax.fori_loop(0, VOCAB_LOCAL // VOCAB_STEP, turn_head, 0)
    drain(w_cols.at[:, half], recvs.at[11])
    drain(head_all, recvs.at[3])

    terms = jnp.dot(
        spread(head_all[...]), w_cols[...].reshape(D, ROWS), preferred_element_type=F32
    )
    wide = stream_all[:, :, pl.ds(pl.multiple_of(me * ROWS, ROWS), ROWS)].astype(F32)
    after_own[...] = (wide + terms.reshape(TENSOR, OWN, ROWS)).astype(BF16)
    cross(4, lambda there: after_own, after_all.at[me], after_all)
    ready(6, 7, 8, 9)
    drain(after_all, recvs.at[4])
    own = after_all.at[:, me]
    send(own, after_rows, sends.at[8], recvs.at[8], {"guide": other})
    finish.append(lambda: drain(after_rows, sends.at[8]))

    wide = jnp.concatenate(
        [after_all[k].astype(F32).reshape(ROWS, ROWS) for k in range(TENSOR)], axis=1
    )
    rows = rms_norm(wide, gains_v[1]).astype(BF16)
    gate = jnp.dot(rows, w_gate_v[...], preferred_element_type=F32)
    upward = jnp.dot(rows, w_up_v[...], preferred_element_type=F32)
    hidden = (gate * jax.nn.sigmoid(gate) * upward).astype(BF16)
    terms = jnp.dot(hidden, w_down_v[...], preferred_element_type=F32)
    partial[...] = terms.reshape(TENSOR, OWN, D).astype(BF16)
    cross(5, lambda there: partial.at[there], shares.at[me], shares)
    drain(after_rows, recvs.at[8])
    wide = jnp.concatenate([after_rows[k].astype(F32) for k in range(TENSOR)], axis=1)
    drain(shares, recvs.at[5])
    share = shares[0].astype(F32)
    for k in range(1, TENSOR):
        share = share + shares[k].astype(F32)
    layer_own[...] = (wide + share).astype(BF16)
    cross(6, lambda there: layer_own, layer_all.at[other, me], layer_all.at[other])

    request = batch * ROWS + lax.broadcasted_iota(jnp.int32, (ROWS, VOCAB_STEP), 0)
    level = jnp.full((ROWS, VOCAB_STEP), levels[0].astype(F32))
    bound = counts[0]
    for t in range(1, TENANTS):
        level = jnp.where(request >= bound, levels[t].astype(F32), level)
        bound = bound + counts[t]
    weight = level * 0.25
    ready(10, 11, 12)

    def arrive(branch):
        @pl.when(guide == branch)
        def _():
            drain(layer_all.at[branch], recvs.at[6])
            send(layer_all.at[branch], layer_all.at[branch], sends.at[9], recvs.at[9], {"guide": other})

        pl.when(guide != branch)(lambda: drain(layer_all.at[branch], recvs.at[9]))
        for at in range(0, TENSOR, SIDE):
            wide = layer_all[branch, at : at + SIDE].astype(F32).reshape(SIDE * OWN, D)
            final_rows[at * OWN : (at + SIDE) * OWN] = rms_norm(wide, gains_v[3]).astype(BF16)

    def logits(step):
        return jnp.dot(
            final_rows[...], lm_head_t[:, step * VOCAB_STEP : (step + 1) * VOCAB_STEP],
            preferred_element_type=F32,
        )

    steps = VOCAB_LOCAL // VOCAB_STEP
    arrive(0)
    for step in range(steps):
        cond_all[:, step * VOCAB_STEP : (step + 1) * VOCAB_STEP] = logits(step)
    arrive(1)
    finish.append(lambda: drain(layer_all.at[0], sends.at[9]))
    top = jnp.full((ROWS, VOCAB_STEP), -jnp.inf, F32)
    for step in range(steps):
        here = slice(step * VOCAB_STEP, (step + 1) * VOCAB_STEP)
        uncond = logits(step)
        guided = uncond + weight * (cond_all[:, here] - uncond)
        cond_all[:, here] = guided
        top = jnp.maximum(top, guided)
        copy = pltpu.make_async_copy(cond_all.at[:, here], guided_all.at[:, here], load_sems.at[step])
        copy.start()
        finish.append(copy.wait)
    top = jnp.max(top, axis=1, keepdims=True)
    mass = jnp.zeros((ROWS, VOCAB_STEP), F32)
    for step in range(steps):
        mass = mass + jnp.exp(cond_all[:, step * VOCAB_STEP : (step + 1) * VOCAB_STEP] - top)
    mass = jnp.sum(mass, axis=1, keepdims=True)
    column = lax.broadcasted_iota(jnp.int32, (ROWS, ROWS), 1)
    packed = jnp.where(column == 0, top, mass)
    place = guide * TENSOR + me
    mine = jnp.transpose(packed)[0:8]
    stats_own[...] = mine
    stats_all[place] = mine
    for there in chips:
        send(stats_own, stats_all.at[place], sends.at[7], recvs.at[7], {"guide": other, "tensor": there})
    for there in chips[:-1]:
        send(stats_own, stats_all.at[place], sends.at[7], recvs.at[7], {"tensor": there})
    finish.append(lambda: drain(stats_all.at[pl.ds(0, GUIDE * TENSOR - 1)], sends.at[7]))

    copy = pltpu.make_async_copy(layer_all.at[guide, me], layer_out, load_sems.at[steps])
    copy.start()
    finish.append(copy.wait)
    for at in range(0, TENSOR, SIDE):
        wide = layer_all[guide, pl.ds(at, SIDE)].astype(F32).reshape(SIDE * OWN, D)
        final_rows[at * OWN : (at + SIDE) * OWN] = rms_norm(wide, gains_v[2]).astype(BF16)
    next_own[...] = lax.dot_general(
        w_next_v[...], final_rows[...], NT, preferred_element_type=F32
    ).astype(BF16)
    copy = pltpu.make_async_copy(next_own, next_qkv, load_sems.at[steps + 1])
    copy.start()
    finish.append(copy.wait)
    drain(stats_all.at[pl.ds(0, GUIDE * TENSOR - 1)], recvs.at[7])
    peaks = stats_all[:, 0, :]
    peak = jnp.max(peaks, axis=0, keepdims=True)
    total = jnp.sum(stats_all[:, 1, :] * jnp.exp(peaks - peak), axis=0, keepdims=True)
    level_out[...] = jnp.transpose(jnp.broadcast_to(peak + jnp.log(total), (ROWS, ROWS)))

    for last in finish:
        last()


def settle(guided, level, layer_rows, next_rows, logprobs, layer_out, next_qkv):
    layer_out[...] = layer_rows[...]
    next_qkv[...] = next_rows[...]
    wide = jnp.concatenate([level[...]] * (VOCAB_LOCAL // ROWS), axis=1)
    logprobs[...] = guided[...] - wide


def local(
    stream, attn_gain, w_qkv, cache_keys, cache_values, cache_len, w_out, mlp_gain, w_gate, w_up, w_down,
    final_gain, lm_head, next_gain, w_next, tenant_counts, guide_level,
):
    hbm = pl.BlockSpec(memory_space=pl.ANY)
    smem = pl.BlockSpec(memory_space=pltpu.SMEM)
    vmem = pl.BlockSpec(memory_space=pltpu.VMEM)
    dma = pltpu.SemaphoreType.DMA
    wide = lambda gain: gain.reshape(1, D)
    guided, level, layer_rows, next_rows = pl.pallas_call(
        kernel,
        name="decode_step",
        out_shape=(
            jax.ShapeDtypeStruct((ROWS, VOCAB_LOCAL), F32),
            jax.ShapeDtypeStruct((ROWS, ROWS), F32),
            jax.ShapeDtypeStruct((OWN, D), BF16),
            jax.ShapeDtypeStruct((QKV_LOCAL, ROWS), BF16),
        ),
        in_specs=[hbm] * 5 + [smem] + [hbm] * 9 + [smem] * 2,
        out_specs=(hbm, vmem, hbm, hbm),
        scratch_shapes=[
            pltpu.VMEM((OWN, D), BF16),
            pltpu.VMEM((4, 1, D), F32),
            pltpu.VMEM((QKV_LOCAL, D), BF16),
            pltpu.VMEM((OWN, SLOTS, KV_WIDTH), BF16),
            pltpu.VMEM((OWN, SLOTS, KV_WIDTH), BF16),
            pltpu.VMEM((ROWS, D), BF16),
            pltpu.VMEM((D, FF_LOCAL), BF16),
            pltpu.VMEM((D, FF_LOCAL), BF16),
            pltpu.VMEM((FF_LOCAL, D), BF16),
            pltpu.VMEM((VOCAB_LOCAL, D), BF16),
            pltpu.VMEM((QKV_LOCAL, D), BF16),
            pltpu.VMEM((D, VOCAB_LOCAL), BF16),
            pltpu.VMEM((TENSOR, OWN, D), BF16),
            pltpu.VMEM((TENSOR, OWN, QKV_LOCAL), BF16),
            pltpu.VMEM((TENSOR, OWN, QKV_LOCAL), BF16),
            pltpu.VMEM((GROUPS + 2, OWN, KV_WIDTH), F32),
            pltpu.VMEM((OWN, HEADS, SLOTS), F32),
            pltpu.VMEM((OWN, HEADS, SLOTS), BF16),
            pltpu.VMEM((GROUPS, OWN, KV_WIDTH), F32),
            pltpu.VMEM((OWN, D), BF16),
            pltpu.VMEM((TENSOR, OWN, D), BF16),
            pltpu.VMEM((TENSOR, ROWS, ROWS), BF16),
            pltpu.VMEM((TENSOR, OWN, ROWS), BF16),
            pltpu.VMEM((TENSOR, TENSOR, OWN, ROWS), BF16),
            pltpu.VMEM((TENSOR, OWN, ROWS), BF16),
            pltpu.VMEM((TENSOR, OWN, D), BF16),
            pltpu.VMEM((TENSOR, OWN, D), BF16),
            pltpu.VMEM((OWN, D), BF16),
            pltpu.VMEM((GUIDE, TENSOR, OWN, D), BF16),
            pltpu.VMEM((ROWS, D), BF16),
            pltpu.VMEM((ROWS, VOCAB_LOCAL), F32),
            pltpu.VMEM((QKV_LOCAL, ROWS), BF16),
            pltpu.VMEM((8, ROWS), F32),
            pltpu.VMEM((GUIDE * TENSOR, 8, ROWS), F32),
            dma((14,)),
            dma((12,)),
            dma((12,)),
        ],
        compiler_params=pltpu.CompilerParams(
            collective_id=0, has_side_effects=True, vmem_limit_bytes=60 * 1024 * 1024
        ),
    )(
        stream, wide(attn_gain), w_qkv.T, cache_keys, cache_values, cache_len, w_out, wide(mlp_gain),
        w_gate, w_up, w_down, wide(final_gain), lm_head, wide(next_gain), w_next.T, tenant_counts, guide_level,
    )

    logprobs, layer_out, next_qkv = pl.pallas_call(
        settle,
        name="settle",
        out_shape=(
            jax.ShapeDtypeStruct((ROWS, VOCAB_LOCAL), F32),
            jax.ShapeDtypeStruct((OWN, D), BF16),
            jax.ShapeDtypeStruct((QKV_LOCAL, ROWS), BF16),
        ),
        in_specs=[vmem] * 4,
        out_specs=(vmem, vmem, vmem),
    )(guided, level, layer_rows, next_rows)
    return logprobs, layer_out[None], next_qkv.T[None]


def solution(mesh):
    in_specs = (
        P("guide", ("batch", "tensor"), None),
        P(),
        P(None, "tensor"),
        P("guide", ("batch", "tensor"), None, None),
        P("guide", ("batch", "tensor"), None, None),
        P("guide", ("batch", "tensor")),
        P("tensor", None),
        P(),
        P(None, "tensor"),
        P(None, "tensor"),
        P("tensor", None),
        P(),
        P(("guide", "tensor"), None),
        P(),
        P(None, "tensor"),
        P(),
        P(),
    )
    out_specs = (
        P("batch", ("guide", "tensor")),
        P("guide", ("batch", "tensor"), None),
        P("guide", "batch", "tensor"),
    )
    return jax.shard_map(local, mesh=mesh, in_specs=in_specs, out_specs=out_specs, check_vma=False)
```

```python
import functools
import math

import jax
import jax.numpy as jnp
from jax import lax
from jax.experimental import pallas as pl
from jax.experimental.pallas import tpu as pltpu
from jax.sharding import PartitionSpec as P

D = 2048
HEADS = 32
KV_HEADS = 8
GROUPS = HEADS // KV_HEADS
HEAD_DIM = 64
KV_WIDTH = KV_HEADS * HEAD_DIM
TENANTS = 4
SLOTS = 1024
FF_LOCAL = 512
QKV_LOCAL = 192
VOCAB_LOCAL = 2048
ROWS = 128
OWN = 8
SIDE = 4
TENSOR = 16
GUIDE = 2
VOCAB_STEP = 512

EPSILON = 1e-05
ROPE_BASE = 500000.0
MASKED = -1e30
MESH = pl.DeviceIdType.MESH
F32 = jnp.float32
BF16 = jnp.bfloat16
NT = (((1,), (1,)), ((), ()))


def norm_factor(wide):
    return lax.rsqrt(jnp.mean(wide * wide, axis=-1, keepdims=True) + EPSILON)


def rms_norm(wide, gain):
    return wide * norm_factor(wide) * gain


def lane_freq(shape):
    lane = lax.broadcasted_iota(jnp.int32, shape, 1)
    steps_up = (lane % (HEAD_DIM // 2)).astype(F32)
    base_freq = jnp.exp(steps_up * (-2.0 * math.log(ROPE_BASE) / HEAD_DIM))
    wavelen = 2.0 * math.pi / base_freq
    smooth = (8192.0 / wavelen - 1.0) / 3.0
    middle = (1.0 - smooth) * base_freq / 32.0 + smooth * base_freq
    return jnp.where(
        wavelen < 2048.0, base_freq, jnp.where(wavelen > 8192.0, base_freq / 32.0, middle)
    )


def rotate(wide, cosine, sine, first):
    width = wide.shape[-1]
    ahead = pltpu.roll(wide, width - HEAD_DIM // 2, 1)
    behind = pltpu.roll(wide, HEAD_DIM // 2, 1)
    return wide * cosine + jnp.where(first, -ahead, behind) * sine


def spread(block):
    return block.astype(F32).reshape(-1, block.shape[-1]).astype(BF16)


def drain(ref, sem):
    pltpu.make_async_copy(ref, ref, sem).wait()


def send(src, dst, send_sem, recv_sem, device):
    pltpu.make_async_remote_copy(
        src_ref=src,
        dst_ref=dst,
        send_sem=send_sem,
        recv_sem=recv_sem,
        device_id=device,
        device_id_type=MESH,
    ).start()


OFFSETS = (
    (2, 2), (1, 2), (2, 1), (3, 2), (2, 3), (1, 1), (3, 3), (1, 3), (3, 1),
    (0, 2), (2, 0), (0, 1), (1, 0), (0, 3), (3, 0), (0, 0),
)

FAR = 5


def kernel(
    stream, attn_gain, w_qkv, keys, values, lengths, w_out, mlp_gain, w_gate, w_up, w_down,
    final_gain, lm_head, next_gain, w_next, counts, levels,
    guided_all, level_out, layer_out, next_qkv,
    stream_v, gains_v, w_qkv_v, keys_v, values_v, w_out_v, w_gate_v, w_up_v, w_down_v, lm_head_v, w_next_v,
    lm_head_t, stream_all, proj, request_side, queries, scores, probs, mixed, head_out, head_all, w_cols, after_own, after_all, after_rows,
    partial, shares, layer_own, layer_all, final_rows, cond_all, next_own, stats_own, stats_all,
    load_sems, sends, recvs,
):
    guide = lax.axis_index("guide")
    me = lax.axis_index("tensor")
    batch = lax.axis_index("batch")
    y = me // SIDE
    x = lax.rem(me, SIDE)
    other = 1 - guide
    chips = [lax.rem(y + dy, SIDE) * SIDE + lax.rem(x + dx, SIDE) for dy, dx in OFFSETS]

    barrier = pltpu.get_barrier_semaphore()
    for there in chips:
        pl.semaphore_signal(
            barrier, inc=1, device_id={"guide": other, "tensor": there}, device_id_type=MESH
        )
    for there in chips[:-1]:
        pl.semaphore_signal(barrier, inc=1, device_id={"tensor": there}, device_id_type=MESH)

    loads = [
        pltpu.make_async_copy(stream.at[0], stream_v, load_sems.at[0]),
        pltpu.make_async_copy(attn_gain, gains_v.at[0], load_sems.at[1]),
        pltpu.make_async_copy(w_qkv, w_qkv_v, load_sems.at[2]),
        pltpu.make_async_copy(w_out, w_out_v, load_sems.at[3]),
        pltpu.make_async_copy(keys.at[0], keys_v, load_sems.at[4]),
        pltpu.make_async_copy(values.at[0], values_v, load_sems.at[5]),
        pltpu.make_async_copy(mlp_gain, gains_v.at[1], load_sems.at[6]),
        pltpu.make_async_copy(w_gate, w_gate_v, load_sems.at[7]),
        pltpu.make_async_copy(w_up, w_up_v, load_sems.at[8]),
        pltpu.make_async_copy(w_down, w_down_v, load_sems.at[9]),
        pltpu.make_async_copy(next_gain, gains_v.at[2], load_sems.at[10]),
        pltpu.make_async_copy(final_gain, gains_v.at[3], load_sems.at[11]),
        pltpu.make_async_copy(w_next, w_next_v, load_sems.at[12]),
        pltpu.make_async_copy(lm_head, lm_head_v, load_sems.at[13]),
    ]
    for load in loads:
        load.start()
    left = dict(enumerate(loads))
    finish = []

    def ready(*which):
        for k in which:
            left.pop(k).wait()

    def cross(phase, part, dst, whole, early=(), apart=10):
        for offset, there in zip(OFFSETS, chips):
            landed = recvs.at[apart] if offset in early else recvs.at[phase]
            send(part(there), dst, sends.at[phase], landed, {"guide": other, "tensor": there})
        finish.append(lambda: drain(whole, sends.at[phase]))

    pl.semaphore_wait(barrier, 2 * TENSOR - 1)
    ready(0)
    pl.when(guide == 1)(lambda: drain(stream_all.at[0], recvs.at[10]))
    cross(0, lambda there: stream_v, stream_all.at[me], stream_all, early=((0, 1),))
    pl.when(guide == 0)(lambda: drain(stream_all.at[0], recvs.at[10]))

    row = lax.broadcasted_iota(jnp.int32, (OWN, 2 * HEAD_DIM), 0)
    position = jnp.zeros((OWN, 2 * HEAD_DIM), F32)
    for r in range(OWN):
        position = jnp.where(row == r, lengths[0, r].astype(F32), position)
    angle = position * lane_freq((OWN, 2 * HEAD_DIM))
    cosine = jnp.concatenate([jnp.cos(angle)] * (KV_WIDTH // (2 * HEAD_DIM)), axis=1)
    sine = jnp.concatenate([jnp.sin(angle)] * (KV_WIDTH // (2 * HEAD_DIM)), axis=1)
    ready(1, 2, 3)
    drain(stream_all.at[pl.ds(0, TENSOR - 1)], recvs.at[0])

    wide = stream_all[...].astype(F32).reshape(ROWS, D)
    rows = rms_norm(wide, gains_v[0]).astype(BF16)
    projected = lax.dot_general(rows, w_qkv_v[...], NT, preferred_element_type=F32)
    proj[:, :, 0:QKV_LOCAL] = projected.reshape(TENSOR, OWN, QKV_LOCAL).astype(BF16)
    cross(1, lambda there: proj.at[there], request_side.at[me], request_side)
    half = pl.ds(pl.multiple_of(guide * (ROWS // 2), ROWS // 2), ROWS // 2)
    rest = pl.ds(pl.multiple_of(other * (ROWS // 2), ROWS // 2), ROWS // 2)
    cross(
        2,
        lambda there: w_out_v.at[half, pl.ds(pl.multiple_of(there * ROWS, ROWS), ROWS)],
        w_cols.at[me, half],
        w_cols.at[:, half],
    )
    drain(request_side, recvs.at[1])

    def piece(column):
        at, j = divmod(column, 3)
        return request_side[at, :, j * HEAD_DIM : (j + 1) * HEAD_DIM].astype(F32)

    lane = lax.broadcasted_iota(jnp.int32, (OWN, KV_WIDTH), 1)
    first = lax.rem(lane, HEAD_DIM) < HEAD_DIM // 2
    for g in range(GROUPS):
        wide = jnp.concatenate([piece(GROUPS * k + g) for k in range(KV_HEADS)], axis=1)
        queries[g] = rotate(wide, cosine, sine, first).astype(BF16).astype(F32) * (HEAD_DIM**-0.5)
    wide = jnp.concatenate([piece(HEADS + k) for k in range(KV_HEADS)], axis=1)
    queries[GROUPS] = rotate(wide, cosine, sine, first).astype(BF16).astype(F32)
    queries[GROUPS + 1] = jnp.concatenate(
        [piece(HEADS + KV_HEADS + k) for k in range(KV_HEADS)], axis=1
    )

    ready(4, 5)
    own_head = lane // HEAD_DIM == lax.broadcasted_iota(jnp.int32, (OWN, KV_WIDTH), 0)
    slot = lax.broadcasted_iota(jnp.int32, (HEADS, SLOTS), 1)

    fresh = []
    for r in range(OWN):
        spread_q = jnp.concatenate(
            [
                jnp.where(own_head, jnp.broadcast_to(queries[g, r : r + 1, :], (KV_HEADS, KV_WIDTH)), 0.0)
                for g in range(GROUPS)
            ],
            axis=0,
        )
        scores[r] = lax.dot_general(spread_q.astype(BF16), keys_v[r], NT, preferred_element_type=F32)
        fresh.append(jnp.sum(spread_q * queries[GROUPS, r : r + 1, :], axis=1, keepdims=True))
    drain(w_cols.at[:, rest], recvs.at[2])
    send(w_cols.at[:, rest], w_cols.at[:, rest], sends.at[11], recvs.at[11], {"guide": other})
    finish.append(lambda: drain(w_cols.at[:, rest], sends.at[11]))
    totals = []
    for r in range(OWN):
        masked = jnp.where(slot < lengths[0, r], scores[r], MASKED)
        peak = jnp.maximum(jnp.max(masked, axis=1, keepdims=True), fresh[r])
        expd = jnp.exp(masked - peak)
        fresh[r] = jnp.exp(fresh[r] - peak)
        totals.append(jnp.sum(expd, axis=1, keepdims=True) + fresh[r])
        probs[r] = expd.astype(BF16)
    for r in range(OWN):
        weighted = jnp.dot(probs[r], values_v[r], preferred_element_type=F32)
        weighted = weighted + fresh[r].astype(BF16).astype(F32) * queries[GROUPS + 1, r : r + 1, :]
        weighted = weighted / totals[r]
        for g in range(GROUPS):
            kept = jnp.where(own_head, weighted[g * KV_HEADS : (g + 1) * KV_HEADS], 0.0)
            mixed[g, r : r + 1, :] = jnp.sum(kept, axis=0, keepdims=True)
    for k in range(KV_HEADS):
        here = slice(k * HEAD_DIM, (k + 1) * HEAD_DIM)
        head_out[:, k * GROUPS * HEAD_DIM : (k + 1) * GROUPS * HEAD_DIM] = jnp.concatenate(
            [mixed[g, :, here] for g in range(GROUPS)], axis=1
        ).astype(BF16)
    cross(3, lambda there: head_out, head_all.at[me], head_all)
    ready(13)

    def turn_head(step, carry):
        here = pl.ds(pl.multiple_of(step * VOCAB_STEP, VOCAB_STEP), VOCAB_STEP)
        lm_head_t[:, here] = lm_head_v[here, :].T
        return carry

    lax.fori_loop(0, VOCAB_LOCAL // VOCAB_STEP, turn_head, 0)
    drain(w_cols.at[:, half], recvs.at[11])
    drain(head_all, recvs.at[3])

    terms = jnp.dot(
        spread(head_all[...]), w_cols[...].reshape(D, ROWS), preferred_element_type=F32
    )
    wide = stream_all[:, :, pl.ds(pl.multiple_of(me * ROWS, ROWS), ROWS)].astype(F32)
    after_own[...] = (wide + terms.reshape(TENSOR, OWN, ROWS)).astype(BF16)
    cross(4, lambda there: after_own, after_all.at[me], after_all)
    ready(6, 7, 8, 9)
    drain(after_all, recvs.at[4])
    own = after_all.at[:, me]
    send(own, after_rows, sends.at[8], recvs.at[8], {"guide": other})
    finish.append(lambda: drain(after_rows, sends.at[8]))

    wide = jnp.concatenate(
        [after_all[k].astype(F32).reshape(ROWS, ROWS) for k in range(TENSOR)], axis=1
    )
    rows = rms_norm(wide, gains_v[1]).astype(BF16)
    gate = jnp.dot(rows, w_gate_v[...], preferred_element_type=F32)
    upward = jnp.dot(rows, w_up_v[...], preferred_element_type=F32)
    hidden = (gate * jax.nn.sigmoid(gate) * upward).astype(BF16)
    terms = jnp.dot(hidden, w_down_v[...], preferred_element_type=F32)
    partial[...] = terms.reshape(TENSOR, OWN, D).astype(BF16)
    cross(5, lambda there: partial.at[there], shares.at[me], shares)
    drain(after_rows, recvs.at[8])
    wide = jnp.concatenate([after_rows[k].astype(F32) for k in range(TENSOR)], axis=1)
    drain(shares, recvs.at[5])
    share = shares[0].astype(F32)
    for k in range(1, TENSOR):
        share = share + shares[k].astype(F32)
    layer_own[...] = (wide + share).astype(BF16)
    cross(
        6, lambda there: layer_own, layer_all.at[other, me], layer_all.at[other],
        early=OFFSETS[FAR:], apart=12,
    )

    request = batch * ROWS + lax.broadcasted_iota(jnp.int32, (ROWS, VOCAB_STEP), 0)
    level = jnp.full((ROWS, VOCAB_STEP), levels[0].astype(F32))
    bound = counts[0]
    for t in range(1, TENANTS):
        level = jnp.where(request >= bound, levels[t].astype(F32), level)
        bound = bound + counts[t]
    weight = level * 0.25
    ready(10, 11, 12)

    def arrive(branch):
        @pl.when(guide == branch)
        def _():
            drain(layer_all.at[branch, pl.ds(FAR, TENSOR - FAR)], recvs.at[12])
            for there in chips[FAR:]:
                block = layer_all.at[branch, there]
                send(block, block, sends.at[9], recvs.at[9], {"guide": other})
            drain(layer_all.at[branch, pl.ds(0, FAR)], recvs.at[6])
            for there in chips[:FAR]:
                block = layer_all.at[branch, there]
                send(block, block, sends.at[9], recvs.at[9], {"guide": other})

        pl.when(guide != branch)(lambda: drain(layer_all.at[branch], recvs.at[9]))
        for at in range(0, TENSOR, SIDE):
            wide = layer_all[branch, at : at + SIDE].astype(F32).reshape(SIDE * OWN, D)
            final_rows[at * OWN : (at + SIDE) * OWN] = rms_norm(wide, gains_v[3]).astype(BF16)

    def logits(step):
        return jnp.dot(
            final_rows[...], lm_head_t[:, step * VOCAB_STEP : (step + 1) * VOCAB_STEP],
            preferred_element_type=F32,
        )

    steps = VOCAB_LOCAL // VOCAB_STEP
    arrive(0)
    for step in range(steps):
        cond_all[:, step * VOCAB_STEP : (step + 1) * VOCAB_STEP] = logits(step)
    arrive(1)
    finish.append(lambda: drain(layer_all.at[0], sends.at[9]))
    top = jnp.full((ROWS, VOCAB_STEP), -jnp.inf, F32)
    for step in range(steps):
        here = slice(step * VOCAB_STEP, (step + 1) * VOCAB_STEP)
        uncond = logits(step)
        guided = uncond + weight * (cond_all[:, here] - uncond)
        cond_all[:, here] = guided
        top = jnp.maximum(top, guided)
        copy = pltpu.make_async_copy(cond_all.at[:, here], guided_all.at[:, here], load_sems.at[step])
        copy.start()
        finish.append(copy.wait)
    top = jnp.max(top, axis=1, keepdims=True)
    mass = jnp.zeros((ROWS, VOCAB_STEP), F32)
    for step in range(steps):
        mass = mass + jnp.exp(cond_all[:, step * VOCAB_STEP : (step + 1) * VOCAB_STEP] - top)
    mass = jnp.sum(mass, axis=1, keepdims=True)
    column = lax.broadcasted_iota(jnp.int32, (ROWS, ROWS), 1)
    packed = jnp.where(column == 0, top, mass)
    place = guide * TENSOR + me
    mine = jnp.transpose(packed)[0:8]
    stats_own[...] = mine
    stats_all[place] = mine
    for there in chips:
        send(stats_own, stats_all.at[place], sends.at[7], recvs.at[7], {"guide": other, "tensor": there})
    for there in chips[:-1]:
        send(stats_own, stats_all.at[place], sends.at[7], recvs.at[7], {"tensor": there})
    finish.append(lambda: drain(stats_all.at[pl.ds(0, GUIDE * TENSOR - 1)], sends.at[7]))

    copy = pltpu.make_async_copy(layer_all.at[guide, me], layer_out, load_sems.at[steps])
    copy.start()
    finish.append(copy.wait)
    for at in range(0, TENSOR, SIDE):
        wide = layer_all[guide, pl.ds(at, SIDE)].astype(F32).reshape(SIDE * OWN, D)
        final_rows[at * OWN : (at + SIDE) * OWN] = rms_norm(wide, gains_v[2]).astype(BF16)
    next_own[...] = lax.dot_general(
        w_next_v[...], final_rows[...], NT, preferred_element_type=F32
    ).astype(BF16)
    copy = pltpu.make_async_copy(next_own, next_qkv, load_sems.at[steps + 1])
    copy.start()
    finish.append(copy.wait)
    drain(stats_all.at[pl.ds(0, GUIDE * TENSOR - 1)], recvs.at[7])
    peaks = stats_all[:, 0, :]
    peak = jnp.max(peaks, axis=0, keepdims=True)
    total = jnp.sum(stats_all[:, 1, :] * jnp.exp(peaks - peak), axis=0, keepdims=True)
    level_out[...] = jnp.transpose(jnp.broadcast_to(peak + jnp.log(total), (ROWS, ROWS)))

    for last in finish:
        last()


def settle(guided, level, layer_rows, next_rows, logprobs, layer_out, next_qkv):
    layer_out[...] = layer_rows[...]
    next_qkv[...] = next_rows[...]
    wide = jnp.concatenate([level[...]] * (VOCAB_LOCAL // ROWS), axis=1)
    logprobs[...] = guided[...] - wide


def local(
    stream, attn_gain, w_qkv, cache_keys, cache_values, cache_len, w_out, mlp_gain, w_gate, w_up, w_down,
    final_gain, lm_head, next_gain, w_next, tenant_counts, guide_level,
):
    hbm = pl.BlockSpec(memory_space=pl.ANY)
    smem = pl.BlockSpec(memory_space=pltpu.SMEM)
    vmem = pl.BlockSpec(memory_space=pltpu.VMEM)
    dma = pltpu.SemaphoreType.DMA
    wide = lambda gain: gain.reshape(1, D)
    guided, level, layer_rows, next_rows = pl.pallas_call(
        kernel,
        name="decode_step",
        out_shape=(
            jax.ShapeDtypeStruct((ROWS, VOCAB_LOCAL), F32),
            jax.ShapeDtypeStruct((ROWS, ROWS), F32),
            jax.ShapeDtypeStruct((OWN, D), BF16),
            jax.ShapeDtypeStruct((QKV_LOCAL, ROWS), BF16),
        ),
        in_specs=[hbm] * 5 + [smem] + [hbm] * 9 + [smem] * 2,
        out_specs=(hbm, vmem, hbm, hbm),
        scratch_shapes=[
            pltpu.VMEM((OWN, D), BF16),
            pltpu.VMEM((4, 1, D), F32),
            pltpu.VMEM((QKV_LOCAL, D), BF16),
            pltpu.VMEM((OWN, SLOTS, KV_WIDTH), BF16),
            pltpu.VMEM((OWN, SLOTS, KV_WIDTH), BF16),
            pltpu.VMEM((ROWS, D), BF16),
            pltpu.VMEM((D, FF_LOCAL), BF16),
            pltpu.VMEM((D, FF_LOCAL), BF16),
            pltpu.VMEM((FF_LOCAL, D), BF16),
            pltpu.VMEM((VOCAB_LOCAL, D), BF16),
            pltpu.VMEM((QKV_LOCAL, D), BF16),
            pltpu.VMEM((D, VOCAB_LOCAL), BF16),
            pltpu.VMEM((TENSOR, OWN, D), BF16),
            pltpu.VMEM((TENSOR, OWN, QKV_LOCAL), BF16),
            pltpu.VMEM((TENSOR, OWN, QKV_LOCAL), BF16),
            pltpu.VMEM((GROUPS + 2, OWN, KV_WIDTH), F32),
            pltpu.VMEM((OWN, HEADS, SLOTS), F32),
            pltpu.VMEM((OWN, HEADS, SLOTS), BF16),
            pltpu.VMEM((GROUPS, OWN, KV_WIDTH), F32),
            pltpu.VMEM((OWN, D), BF16),
            pltpu.VMEM((TENSOR, OWN, D), BF16),
            pltpu.VMEM((TENSOR, ROWS, ROWS), BF16),
            pltpu.VMEM((TENSOR, OWN, ROWS), BF16),
            pltpu.VMEM((TENSOR, TENSOR, OWN, ROWS), BF16),
            pltpu.VMEM((TENSOR, OWN, ROWS), BF16),
            pltpu.VMEM((TENSOR, OWN, D), BF16),
            pltpu.VMEM((TENSOR, OWN, D), BF16),
            pltpu.VMEM((OWN, D), BF16),
            pltpu.VMEM((GUIDE, TENSOR, OWN, D), BF16),
            pltpu.VMEM((ROWS, D), BF16),
            pltpu.VMEM((ROWS, VOCAB_LOCAL), F32),
            pltpu.VMEM((QKV_LOCAL, ROWS), BF16),
            pltpu.VMEM((8, ROWS), F32),
            pltpu.VMEM((GUIDE * TENSOR, 8, ROWS), F32),
            dma((14,)),
            dma((12,)),
            dma((13,)),
        ],
        compiler_params=pltpu.CompilerParams(
            collective_id=0, has_side_effects=True, vmem_limit_bytes=60 * 1024 * 1024
        ),
    )(
        stream, wide(attn_gain), w_qkv.T, cache_keys, cache_values, cache_len, w_out, wide(mlp_gain),
        w_gate, w_up, w_down, wide(final_gain), lm_head, wide(next_gain), w_next.T, tenant_counts, guide_level,
    )

    logprobs, layer_out, next_qkv = pl.pallas_call(
        settle,
        name="settle",
        out_shape=(
            jax.ShapeDtypeStruct((ROWS, VOCAB_LOCAL), F32),
            jax.ShapeDtypeStruct((OWN, D), BF16),
            jax.ShapeDtypeStruct((QKV_LOCAL, ROWS), BF16),
        ),
        in_specs=[vmem] * 4,
        out_specs=(vmem, vmem, vmem),
    )(guided, level, layer_rows, next_rows)
    return logprobs, layer_out[None], next_qkv.T[None]


def solution(mesh):
    in_specs = (
        P("guide", ("batch", "tensor"), None),
        P(),
        P(None, "tensor"),
        P("guide", ("batch", "tensor"), None, None),
        P("guide", ("batch", "tensor"), None, None),
        P("guide", ("batch", "tensor")),
        P("tensor", None),
        P(),
        P(None, "tensor"),
        P(None, "tensor"),
        P("tensor", None),
        P(),
        P(("guide", "tensor"), None),
        P(),
        P(None, "tensor"),
        P(),
        P(),
    )
    out_specs = (
        P("batch", ("guide", "tensor")),
        P("guide", ("batch", "tensor"), None),
        P("guide", "batch", "tensor"),
    )
    return jax.shard_map(local, mesh=mesh, in_specs=in_specs, out_specs=out_specs, check_vma=False)
```
